32 devices in a mesh: dp: 8 (over y, x, core), fsdp: 4 (over z).
Axes of the slice: x: 2, y: 2, z: 4, core: 2. Of those that a mesh axis runs over, the one named last changes fastest.
Arguments:
- states_in: bfloat16 [16, 256, 2048], P('dp', 'fsdp'), may hold values from -6 to 6
- out_cotangent: bfloat16 [16, 256, 2048], P('dp', 'fsdp'), may hold values from -6 to 6
- segments: int32 [16, 256], P('dp'), may hold values from 0 to 31, as said below
- starts: int32 [16, 256], P('dp'), may hold values from 0 to 1
- norm_gain: bfloat16 [2048], replicated, may hold values from 0.5 to 1.5
- in_x_weight: bfloat16 [2048, 4096], P(None, 'fsdp'), may hold values from -0.125 to 0.125
- in_z_weight: bfloat16 [2048, 4096], P(None, 'fsdp'), may hold values from -0.125 to 0.125
- conv_weight: bfloat16 [4, 4096], P(None, 'fsdp'), may hold values from -3 to 3
- conv_bias: bfloat16 [4096], P('fsdp'), may hold values from -0.5 to 0.5
- x_proj_weight: bfloat16 [4096, 160], P('fsdp'), may hold values from -0.09375 to 0.09375
- dt_weight: bfloat16 [128, 4096], P(None, 'fsdp'), may hold values from -0.5 to 0.5
- dt_bias: bfloat16 [4096], P('fsdp'), may hold values from -4 to 0
- skip_weight: bfloat16 [4096], P('fsdp'), may hold values from 0.5 to 1.5
- out_weight: bfloat16 [4096, 2048], P('fsdp'), may hold values from -0.1875 to 0.1875
Outputs:
- output: bfloat16 [16, 256, 2048], P('dp', 'fsdp')
- input_grad: float32 [16, 256, 2048], P('dp', 'fsdp')
- norm_gain_grad: float32 [2048], replicated
- in_x_grad: float32 [2048, 4096], P('dp', 'fsdp')
- in_z_grad: float32 [2048, 4096], P('dp', 'fsdp')
- conv_grad: float32 [4, 4096], P(None, 'fsdp')
- conv_bias_grad: float32 [4096], P('fsdp')
- x_proj_grad: float32 [4096, 160], P('fsdp')
- dt_grad: float32 [128, 4096], P('dp', 'fsdp')
- dt_bias_grad: float32 [4096], P('fsdp')
- skip_grad: float32 [4096], P('fsdp')
- out_grad: float32 [4096, 2048], P('fsdp', 'dp')
The draws below stay inside these ranges and needn't reach their ends.
Inputs may be any that keep to these rules, and one draw needn't show every extreme that they name: Within each sequence, segments start at 0 at its first token, never fall, and rise by one exactly at the tokens where starts is 1; starts is 1 at every sequence's first token, and 1 only at positions that are multiples of 8.
All inputs are finite; a program needn't handle non-finite values.
Results may differ from the reference program's by a relative error of at most 0.012.
Values may be sent and summed in bfloat16 or wider, within the bound.
No kernel may reach another device: no remote copies, remote signals or barrier semaphores. Data moves between devices by JAX's collectives and lax.ppermute only.
A program may use at most 224 MiB of HBM per device.

```python
import jax
import jax.numpy as jnp
from jax import lax

D = 2048
INNER = 4096
STATE = 16
DT_RANK = 128
CONV = 4
BLOCK = 16
XW = 160
SEQ = 256
BATCH = 16


def document_starts(key):
    level_key, flag_key, row_key = jax.random.split(jax.random.fold_in(key, 11), 3)
    level = jax.random.randint(level_key, (BATCH, 1), 0, 8)
    spacing = jnp.left_shift(jnp.ones((BATCH, 1), jnp.int32), level)
    draws = jax.random.randint(flag_key, (BATCH, SEQ), 0, 1 << 20)
    aligned = (jnp.arange(SEQ) % 8 == 0).astype(jnp.int32)[None, :]
    flags = (draws % spacing == 0).astype(jnp.int32) * aligned
    full_row = jax.random.randint(row_key, (), 0, BATCH)
    chosen = (jnp.arange(BATCH) == full_row).astype(jnp.int32)[:, None] * aligned
    first = (jnp.arange(SEQ) == 0).astype(jnp.int32)[None, :]
    return jnp.maximum(jnp.maximum(flags, chosen), first)


def draw_segments(key, part):
    return (jnp.cumsum(document_starts(key), axis=1) - 1).astype(jnp.int32)


def draw_starts(key, part):
    return document_starts(key)


def level_of(stream_key, dims, cuts, smallest, high):
    loudness, own = 1.0, jax.random.fold_in(stream_key, 6)
    for dim, blocks in cuts:
        steps = jnp.exp(jax.random.uniform(jax.random.fold_in(own, dim), (blocks,), jnp.float32, smallest / len(cuts), high / len(cuts)))
        loudness = loudness * jnp.repeat(steps, dims[dim] // blocks).reshape([-1 if axis == dim else 1 for axis in range(len(dims))])
    return loudness


def centred(own_key, dims, scale, most, pieces=(), held_as=jnp.bfloat16):
    factor_of = level_of(own_key, dims, pieces, -0.22, 0.18) if pieces else 1.0
    values = jax.random.normal(own_key, dims, jnp.float32) * scale * factor_of
    return jnp.minimum(jnp.maximum(values, -most), most).astype(held_as)


def setup_inputs(seed: int = 0) -> dict:
    arg_keys = jax.random.split(jax.random.key(seed), 15)
    states_in = centred(arg_keys[0], (BATCH, SEQ, D), 1.0, 6.0, ((0, 8), (1, 4)))
    out_cotangent = centred(arg_keys[1], (BATCH, SEQ, D), 1.0, 6.0, ((0, 8), (1, 4)))
    segments = draw_segments(jax.random.fold_in(arg_keys[14], 71), 0)
    starts = draw_starts(jax.random.fold_in(arg_keys[14], 71), 0)
    norm_gain = jnp.clip(1.0 + 0.1 * jax.random.normal(arg_keys[4], (D,), jnp.float32), 0.5, 1.5).astype(jnp.bfloat16)
    in_x_weight = centred(arg_keys[5], (D, INNER), D ** -0.5, 0.125, ((1, 4),))
    in_z_weight = centred(arg_keys[6], (D, INNER), D ** -0.5, 0.125, ((1, 4),))
    conv_weight = centred(arg_keys[7], (CONV, INNER), CONV ** -0.5, 3.0, ((1, 4),))
    conv_bias = jnp.clip(jax.random.uniform(arg_keys[8], (INNER,), jnp.float32, -0.5, 0.5) * level_of(arg_keys[8], (INNER,), ((0, 4),), -0.4, 0.0), -0.5, 0.5).astype(jnp.bfloat16)
    x_proj_weight = centred(arg_keys[9], (INNER, XW), INNER ** -0.5, 0.09375, ((0, 4),))
    dt_weight = centred(arg_keys[10], (DT_RANK, INNER), DT_RANK ** -0.5, 0.5, ((1, 4),))
    dt_bias = jnp.clip(-4.0 + 4.0 * jax.random.uniform(arg_keys[11], (INNER,), jnp.float32) ** level_of(arg_keys[11], (INNER,), ((0, 4),), -0.2, 0.2), -4.0, 0.0).astype(jnp.bfloat16)
    skip_weight = jnp.clip(0.5 + 1.0 * jax.random.uniform(arg_keys[12], (INNER,), jnp.float32) ** level_of(arg_keys[12], (INNER,), ((0, 4),), -0.2, 0.2), 0.5, 1.5).astype(jnp.bfloat16)
    out_weight = centred(arg_keys[13], (INNER, D), (INNER // 4) ** -0.5, 0.1875, ((0, 4),))
    return dict(states_in=states_in, out_cotangent=out_cotangent, segments=segments, starts=starts, norm_gain=norm_gain, in_x_weight=in_x_weight, in_z_weight=in_z_weight, conv_weight=conv_weight, conv_bias=conv_bias, x_proj_weight=x_proj_weight, dt_weight=dt_weight, dt_bias=dt_bias, skip_weight=skip_weight, out_weight=out_weight)


norm_eps = 1e-05
highest = lax.Precision.HIGHEST

@jax.custom_vjp
def low(v):
    return lax.optimization_barrier(v.astype(jnp.bfloat16)).astype(jnp.float32)

@jax.custom_vjp
def low_back(v):
    return v

def low_keep(v):
    return (low(v), None)

def low_pass(kept, grad):
    return (grad,)

def back_keep(v):
    return (v, None)

def back_low(kept, grad):
    return (low(grad),)
low.defvjp(low_keep, low_pass)
low_back.defvjp(back_keep, back_low)

def recur_block(state, rates, keys, queries, values, keep):
    scale = rates / (1.0 + rates * lax.optimization_barrier(jnp.sum(keys * keys, axis=1, keepdims=True)))
    results = []
    for position in range(rates.shape[0]):
        column = keys[position][:, None]
        decay = keep[position] * (1.0 - column * column * scale[position][None, :])
        state = decay * state + column * (scale[position] * values[position])[None, :]
        results.append(lax.optimization_barrier(jnp.sum(queries[position][:, None] * state, axis=0)))
    return (jnp.stack(results), state)

def advance(state, block):
    results, state_next = recur_block(state, block[0], block[1], block[2], block[3], block[4])
    return (state_next, results)

def sequence_forward(tokens, params, seg_row, start_row):
    gain, in_x, in_z, taps, bias, proj_w, dt_w, dt_b, skip, out_w = params
    rscale = lax.rsqrt(lax.optimization_barrier(jnp.mean(tokens * tokens, axis=1, keepdims=True)) + norm_eps)
    normed = low(tokens * rscale * gain)
    x_in = low_back(low(jnp.dot(normed, in_x, precision=highest)))
    gate_pre = low_back(jnp.dot(normed, in_z, precision=highest))
    extended = jnp.concatenate([jnp.zeros((CONV - 1, INNER), jnp.float32), x_in], 0)
    seg_ext = jnp.concatenate([jnp.full((CONV - 1,), -1, jnp.int32), seg_row.astype(jnp.int32)], 0)
    conv_pre = bias[None, :]
    for tap in range(CONV):
        same = (seg_ext[tap:tap + SEQ] == seg_ext[CONV - 1:]).astype(jnp.float32)
        conv_pre = conv_pre + taps[tap][None, :] * extended[tap:tap + SEQ] * same[:, None]
    mixer_in = low(jax.nn.silu(conv_pre))
    projected = low_back(jnp.dot(mixer_in, proj_w, precision=highest))
    dt_low = low(projected[:, :DT_RANK])
    keys = projected[:, DT_RANK:DT_RANK + STATE]
    queries = projected[:, DT_RANK + STATE:]
    rates = jax.nn.softplus(low_back(jnp.dot(dt_low, dt_w, precision=highest) + dt_b))
    keep = 1.0 - start_row.astype(jnp.float32)
    blocks = tuple((array.reshape((SEQ // BLOCK, BLOCK) + array.shape[1:]) for array in (rates, keys, queries, mixer_in, keep)))
    _, mixed = lax.scan(jax.checkpoint(advance), jnp.zeros((STATE, INNER), jnp.float32), blocks)
    mixed = mixed.reshape(SEQ, INNER) + skip * mixer_in
    gated = low(mixed * jax.nn.silu(gate_pre))
    return tokens + jnp.dot(gated, out_w, precision=highest)

def reference(states_in, out_cotangent, segments, starts, norm_gain, in_x_weight, in_z_weight, conv_weight, conv_bias, x_proj_weight, dt_weight, dt_bias, skip_weight, out_weight):
    params = tuple((array.astype(jnp.float32) for array in (norm_gain, in_x_weight, in_z_weight, conv_weight, conv_bias, x_proj_weight, dt_weight, dt_bias, skip_weight, out_weight)))

    def one_sequence(totals, item):
        tokens, cotangent, seg_row, start_row = item

        def run(tokens, params):
            return sequence_forward(tokens, params, seg_row, start_row)
        result, back = jax.vjp(run, tokens.astype(jnp.float32), params)
        grad_tokens, grad_params = back(cotangent.astype(jnp.float32))
        totals = tuple((total + grad for total, grad in zip(totals, grad_params)))
        return (totals, (result.astype(jnp.bfloat16), grad_tokens))
    zeros = tuple((jnp.zeros_like(array) for array in params))
    totals, (output, input_grad) = lax.scan(one_sequence, zeros, (states_in, out_cotangent, segments, starts))
    return (output, input_grad, totals[0], totals[1], totals[2], totals[3], totals[4], totals[5], totals[6], totals[7], totals[8], totals[9])
```

```python
import functools

import jax
import jax.numpy as jnp
from jax import lax
from jax.experimental import pallas as pl
from jax.experimental.pallas import tpu as pltpu
from jax.sharding import PartitionSpec as P

BLOCK = 16
LANES = 128
norm_eps = 1e-05
f32 = jnp.float32
bf16 = jnp.bfloat16


def mm(left, right, contract):
    return lax.dot_general(left, right, ((contract[:1], contract[1:]), ((), ())), preferred_element_type=f32)


def swap(x, axis, bit):
    return lax.ppermute(x, axis, [(i, i ^ bit) for i in range(lax.axis_size(axis))])


def bits_of(count):
    return [1 << k for k in range(count.bit_length() - 1)]


def gather_parts(x, axis):
    held = {0: x}
    for bit in reversed(bits_of(lax.axis_size(axis))):
        for mask in list(held):
            held[mask | bit] = swap(held[mask], axis, bit)
    return [held[mask] for mask in range(len(held))]


def take_bit(x, dim, value):
    return lax.dynamic_index_in_dim(x, value, dim, keepdims=False)


class Scatter:
    def __init__(self, x, axis, bits, dims):
        self.x, self.axis, self.left = x, axis, list(zip(bits, dims))

    def send(self):
        bit, dim = self.left[0]
        own = (lax.axis_index(self.axis) // bit) % 2
        self.got = swap(take_bit(self.x, dim, 1 - own).astype(bf16), self.axis, bit)
        self.kept = take_bit(self.x, dim, own)
        return self.got

    def add(self):
        _, dim = self.left.pop(0)
        self.left = [(bit, d - 1 if d > dim else d) for bit, d in self.left]
        self.x = self.kept.astype(f32) + self.got.astype(f32)

    def finish(self):
        while self.left:
            self.send()
            self.add()
        return self.x


def scatter_of(x, axis):
    count = lax.axis_size(axis)
    bits = bits_of(count)
    n = len(bits)
    return Scatter(x.reshape((2,) * n + (x.shape[0] // count,) + x.shape[1:]), axis, bits, range(n - 1, -1, -1))


def scatter_rest(x):
    bits = bits_of(lax.axis_size("dp"))[1:]
    n = len(bits)
    half = x.shape[1] // 2
    parts = []
    for start, order in ((0, list(range(n))), (half, list(range(n))[::-1])):
        piece = x[:, start : start + half].reshape((2,) * n + (half,) + x.shape[2:])
        parts.append(Scatter(piece, "dp", [bits[k] for k in order], [n - 1 - k for k in order]))
    return parts


def all_sum(x, axis, kind=bf16):
    for bit in bits_of(lax.axis_size(axis)):
        low = x.astype(kind)
        x = low.astype(f32) + swap(low, axis, bit).astype(f32)
    return x


def exchange_all(x, axis):
    return [x] + [swap(x, axis, mask) for mask in range(1, lax.axis_size(axis))]


def add_up(refs):
    total = refs[0][...].astype(f32)
    for ref in refs[1:]:
        total = total + ref[...].astype(f32)
    return total


def silu_slope(v):
    s = jax.nn.sigmoid(v)
    return s * (1.0 + v * (1.0 - s))


def conv_sum(x, masks, taps, bias):
    span = taps.shape[0]
    total = bias + taps[span - 1 : span] * x
    shifted = []
    for w in range(span - 1):
        moved = pltpu.roll(x, span - 1 - w, 0) * masks[:, w : w + 1]
        shifted.append(moved)
        total = total + taps[w : w + 1] * moved
    return total, shifted + [x]


def enter_kernel(count, offs_ref, *refs):
    parts = refs[:count]
    gain_ref, mask_ref, wx_ref, wz_ref, taps_ref, bias_ref, wp_ref = refs[count : count + 7]
    normed_ref, xin_ref, z_ref, xs_ref, proj_ref, acc_s = refs[count + 7 :]
    step = pl.program_id(0)

    @pl.when(step == 0)
    def _():
        gain = gain_ref[...].astype(f32)
        for m, part in enumerate(parts):
            v = part[...].astype(f32)
            rscale = lax.rsqrt(jnp.mean(v * v, axis=1, keepdims=True) + norm_eps)
            rows = part.shape[0]
            normed_ref[pl.ds(pl.multiple_of(offs_ref[0, m], rows), rows), :] = (v * rscale * gain).astype(bf16)
        acc_s[...] = jnp.zeros_like(acc_s)

    normed = normed_ref[...]
    z_ref[...] = jnp.dot(normed, wz_ref[...], preferred_element_type=f32)
    x_in = jnp.dot(normed, wx_ref[...], preferred_element_type=f32).astype(bf16)
    xin_ref[...] = x_in
    pre, _ = conv_sum(x_in.astype(f32), mask_ref[...], taps_ref[...].astype(f32), bias_ref[...].astype(f32))
    xs = jax.nn.silu(pre).astype(bf16)
    xs_ref[...] = xs
    acc_s[...] += mm(wp_ref[...], xs, (1, 1))

    @pl.when(step == pl.num_programs(0) - 1)
    def _():
        proj_ref[...] = acc_s[...].astype(bf16)


def blocks_of(rows, wide):
    return pl.BlockSpec((rows, wide), lambda c: (0, c))


def whole_of(shape):
    return pl.BlockSpec(shape, lambda c: (0,) * len(shape))


def enter(offs, parts, gain, masks, wx, wz, taps, bias, wp):
    rows, model = parts[0].shape
    seq_len = rows * len(parts)
    inner = wx.shape[1]
    wide = 256
    return pl.pallas_call(
        functools.partial(enter_kernel, len(parts)),
        grid=(inner // wide,),
        in_specs=[pl.BlockSpec(memory_space=pltpu.SMEM)]
        + [whole_of((rows, model))] * len(parts)
        + [
            whole_of((1, model)),
            whole_of(masks.shape),
            blocks_of(model, wide),
            blocks_of(model, wide),
            blocks_of(taps.shape[0], wide),
            blocks_of(1, wide),
            blocks_of(wp.shape[0], wide),
        ],
        out_specs=[
            whole_of((seq_len, model)),
            blocks_of(seq_len, wide),
            blocks_of(seq_len, wide),
            blocks_of(seq_len, wide),
            whole_of((wp.shape[0], seq_len)),
        ],
        out_shape=[
            jax.ShapeDtypeStruct((seq_len, model), bf16),
            jax.ShapeDtypeStruct((seq_len, inner), bf16),
            jax.ShapeDtypeStruct((seq_len, inner), f32),
            jax.ShapeDtypeStruct((seq_len, inner), bf16),
            jax.ShapeDtypeStruct((wp.shape[0], seq_len), bf16),
        ],
        scratch_shapes=[pltpu.VMEM((wp.shape[0], seq_len), f32)],
        name="enter",
        cost_estimate=pl.CostEstimate(
            flops=4 * seq_len * model * inner,
            bytes_accessed=4 * model * inner + 10 * seq_len * inner,
            transcendentals=seq_len * inner,
        ),
    )(offs, *parts, gain, masks, wx, wz, taps, bias, wp)


def leave_kernel(count, *refs):
    terms = refs[:count]
    wp_ref, gxs_ref, xin_ref, xs_ref, gz_ref, mask_ref, taps_ref, bias_ref, wx_ref, wz_ref, normed_ref = refs[
        count : count + 11
    ]
    gxin_ref, gn_ref, rows_ref, xpg_ref, gain_ref, acc_s = refs[count + 11 :]
    step = pl.program_id(0)
    span = taps_ref.shape[0]
    seq_len = xin_ref.shape[0]
    gproj = add_up(terms).astype(bf16)
    xpg_ref[...] = mm(gproj, xs_ref[...], (1, 0))
    g_xs = gxs_ref[...] + mm(gproj, wp_ref[...], (0, 0))
    masks = mask_ref[...]
    taps = taps_ref[...].astype(f32)
    pre, shifted = conv_sum(xin_ref[...].astype(f32), masks, taps, bias_ref[...].astype(f32))
    g_conv = g_xs * silu_slope(pre)
    total = taps[span - 1 : span] * g_conv
    for w in range(span):
        rows_ref[w : w + 1, :] = jnp.sum(g_conv * shifted[w], axis=0, keepdims=True)
        if w < span - 1:
            term = g_conv * masks[:, w : w + 1] * taps[w : w + 1]
            total = total + pltpu.roll(term, seq_len - (span - 1 - w), 0)
    rows_ref[span : span + 1, :] = jnp.sum(g_conv, axis=0, keepdims=True)
    rows_ref[span + 1 :, :] = jnp.zeros((8 - span - 1, g_conv.shape[1]), f32)
    g_x_in = total.astype(bf16)
    gxin_ref[...] = g_x_in
    gn = mm(g_x_in, wx_ref[...], (1, 1)) + mm(gz_ref[...], wz_ref[...], (1, 1))

    @pl.when(step == 0)
    def _():
        acc_s[...] = gn

    @pl.when(step > 0)
    def _():
        acc_s[...] += gn

    @pl.when(step == pl.num_programs(0) - 1)
    def _():
        gn = acc_s[...]
        gn_ref[...] = gn.astype(bf16)
        gain_ref[...] = jnp.sum(gn * normed_ref[...].astype(f32), axis=0, keepdims=True)


def leave(terms, wp, gxs, xin, xs, gz, masks, taps, bias, wx, wz, normed):
    seq_len, model = normed.shape
    inner = wx.shape[1]
    wide = 256
    return pl.pallas_call(
        functools.partial(leave_kernel, len(terms)),
        grid=(inner // wide,),
        in_specs=[whole_of(terms[0].shape)] * len(terms)
        + [
            blocks_of(wp.shape[0], wide),
            blocks_of(seq_len, wide),
            blocks_of(seq_len, wide),
            blocks_of(seq_len, wide),
            blocks_of(seq_len, wide),
            whole_of(masks.shape),
            blocks_of(taps.shape[0], wide),
            blocks_of(1, wide),
            blocks_of(model, wide),
            blocks_of(model, wide),
            whole_of((seq_len, model)),
        ],
        out_specs=[
            blocks_of(seq_len, wide),
            whole_of((seq_len, model)),
            blocks_of(8, wide),
            blocks_of(wp.shape[0], wide),
            whole_of((1, model)),
        ],
        out_shape=[
            jax.ShapeDtypeStruct((seq_len, inner), bf16),
            jax.ShapeDtypeStruct((seq_len, model), bf16),
            jax.ShapeDtypeStruct((8, inner), f32),
            jax.ShapeDtypeStruct((wp.shape[0], inner), f32),
            jax.ShapeDtypeStruct((1, model), f32),
        ],
        scratch_shapes=[pltpu.VMEM((seq_len, model), f32)],
        name="leave",
        cost_estimate=pl.CostEstimate(
            flops=4 * seq_len * model * inner,
            bytes_accessed=4 * model * inner + 14 * seq_len * inner,
            transcendentals=seq_len * inner,
        ),
    )(*terms, wp, gxs, xin, xs, gz, masks, taps, bias, wx, wz, normed)


def recurrence_kernel(state_dim, rank, count, keep_ref, offs_ref, *refs):
    parts, terms = refs[:count], refs[count : 2 * count]
    xs_ref, z_ref, wo_ref, wdt_ref, dtb_ref, skip_ref = refs[2 * count : 2 * count + 6]
    gated_ref, gz_ref, gxs_ref, gproj_ref, small_ref, dtg_ref, cot_ref, out_ref = refs[2 * count + 6 : 2 * count + 14]
    (
        gg_s,
        proj_s,
        gproj_s,
        acc_s,
        slope_s,
        eps_s,
        u_s,
        gm_s,
        y_s,
        s1_s,
        s2_s,
        hist_s,
        even_g_s,
        odd_g_s,
        even_p_s,
        odd_p_s,
        kt_s,
        qt_s,
        kd_s,
        k2d_s,
        qd_s,
        norm_s,
        sum_s,
        tail_s,
        gq_s,
        ge_s,
        pe_s,
        gqt_s,
        get_s,
        pet_s,
    ) = refs[2 * count + 14 :]
    step = pl.program_id(0)
    seq_len, width = xs_ref.shape
    blocks = seq_len // BLOCK
    flat = BLOCK * state_dim
    lane = lax.broadcasted_iota(jnp.int32, (state_dim, BLOCK), 1)

    @pl.when(step == 0)
    def _():
        proj_s[...] = add_up(terms)
        for m, part in enumerate(parts):
            rows = part.shape[0]
            cot_ref[pl.ds(pl.multiple_of(offs_ref[0, m], rows), rows), :] = part[...]
        turned = proj_s[rank:, :]
        for b in range(blocks):
            cols = slice(b * BLOCK, (b + 1) * BLOCK)
            kt_s[b] = jnp.pad(turned[:state_dim, cols], ((0, 0), (0, LANES - BLOCK)))
            qt_s[b] = jnp.pad(turned[state_dim:, cols], ((0, 0), (0, LANES - BLOCK)))
        source = lax.broadcasted_iota(jnp.int32, (2 * state_dim, flat), 0)
        target = lax.rem(lax.broadcasted_iota(jnp.int32, (2 * state_dim, flat), 1), state_dim)
        take_k = (source == target).astype(bf16)
        take_q = (source == target + state_dim).astype(bf16)
        own = (
            lax.rem(lax.broadcasted_iota(jnp.int32, (seq_len, flat), 0), BLOCK)
            == lax.broadcasted_iota(jnp.int32, (seq_len, flat), 1) // state_dim
        )
        kd_s[...] = jnp.where(own, mm(turned.astype(bf16), take_k, (0, 0)), 0.0).astype(bf16)
        k2d_s[...] = jnp.where(own, mm((turned * turned).astype(bf16), take_k, (0, 0)), 0.0).astype(bf16)
        qd_s[...] = jnp.where(own, mm(turned.astype(bf16), take_q, (0, 0)), 0.0).astype(bf16)
        square = jnp.sum(turned[:state_dim] * turned[:state_dim], axis=0, keepdims=True)
        norm_s[...] = jnp.broadcast_to(square, (LANES, seq_len)).T
        sum_s[...] = jnp.zeros_like(sum_s)
        gq_s[...] = jnp.zeros_like(gq_s)
        ge_s[...] = jnp.zeros_like(ge_s)
        pe_s[...] = jnp.zeros_like(pe_s)

    gg_s[...] = mm(cot_ref[...], wo_ref[...], (1, 1))
    low = proj_s[:rank, :].astype(bf16)
    dt_pre = mm(low, wdt_ref[...], (0, 0)) + dtb_ref[...].astype(f32)
    rates = jnp.maximum(dt_pre, 0.0) + jnp.log1p(jnp.exp(-jnp.abs(dt_pre)))
    ratio = 1.0 / (1.0 + rates * norm_s[:, 0:1])
    eps_s[...] = rates * ratio
    slope_s[...] = ratio * ratio * jax.nn.sigmoid(dt_pre)
    u_s[...] = eps_s[...] * xs_ref[...].astype(f32)
    gm_s[...] = gg_s[...] * jax.nn.silu(z_ref[...])
    hist_s[0:state_dim, :] = jnp.zeros((state_dim, width), bf16)

    def own_token(pairs):
        picked = pairs[:state_dim]
        for t in range(1, BLOCK):
            picked = jnp.where(lane == t, pairs[t * state_dim : (t + 1) * state_dim], picked)
        return picked

    def read_states(b, buf):
        toks = pl.ds(pl.multiple_of(b * BLOCK, BLOCK), BLOCK)
        hblk = buf[...]
        y_s[toks, :] = jnp.dot(qd_s[toks, :], hblk, preferred_element_type=f32)
        gqt_s[b, :, :BLOCK] = own_token(mm(hblk, gm_s[toks, :].astype(bf16), (1, 1)))

    def scan_block(b, h, buf):
        base = pl.multiple_of(b * BLOCK, BLOCK)
        kt = kt_s[b]
        for t in range(BLOCK):
            if t % 8 == 0:
                h = h * keep_ref[0, b * 2 + t // 8]
            col = jnp.broadcast_to(kt[:, t : t + 1], (state_dim, width))
            e = eps_s[pl.ds(base + t, 1), :]
            u = u_s[pl.ds(base + t, 1), :]
            h = (1.0 - (col * col) * e) * h + col * u
            kept = h.astype(bf16)
            hist_s[pl.ds(pl.multiple_of((base + t + 1) * state_dim, state_dim), state_dim), :] = kept
            buf[t * state_dim : (t + 1) * state_dim, :] = kept
        return h

    def forward(i, h):
        read_states(jnp.maximum(2 * i - 1, 0), odd_g_s)
        h = scan_block(2 * i, h, even_g_s)
        read_states(2 * i, even_g_s)
        return scan_block(2 * i + 1, h, odd_g_s)

    lax.fori_loop(0, blocks // 2, forward, jnp.zeros((state_dim, width), f32))
    read_states(blocks - 1, odd_g_s)

    def read_grads(b, gbuf, pbuf):
        toks = pl.ds(pl.multiple_of(b * BLOCK, BLOCK), BLOCK)
        gblk = gbuf[...]
        pblk = pbuf[...]
        s1_s[toks, :] = jnp.dot(kd_s[toks, :], gblk, preferred_element_type=f32)
        s2_s[toks, :] = jnp.dot(k2d_s[toks, :], pblk, preferred_element_type=f32)
        get_s[b, :, :BLOCK] = own_token(mm(gblk, u_s[toks, :].astype(bf16), (1, 1)))
        pet_s[b, :, :BLOCK] = own_token(mm(pblk, eps_s[toks, :].astype(bf16), (1, 1)))

    def back_block(b, carry, gbuf, pbuf):
        base = pl.multiple_of(b * BLOCK, BLOCK)
        kt = kt_s[b]
        qt = qt_s[b]
        for t in reversed(range(BLOCK)):
            colq = jnp.broadcast_to(qt[:, t : t + 1], (state_dim, width))
            col = jnp.broadcast_to(kt[:, t : t + 1], (state_dim, width))
            e = eps_s[pl.ds(base + t, 1), :]
            gm = gm_s[pl.ds(base + t, 1), :]
            g = colq * gm + carry
            before = hist_s[pl.ds(pl.multiple_of((base + t) * state_dim, state_dim), state_dim), :].astype(f32)
            p = g * before
            carry = (1.0 - (col * col) * e) * g
            if t % 8 == 0:
                k = keep_ref[0, b * 2 + t // 8]
                carry = carry * k
                p = p * k
            gbuf[t * state_dim : (t + 1) * state_dim, :] = g.astype(bf16)
            pbuf[t * state_dim : (t + 1) * state_dim, :] = p.astype(bf16)
        return carry

    def backward(i, carry):
        last = blocks - 1 - 2 * i
        read_grads(jnp.minimum(last + 1, blocks - 1), even_g_s, even_p_s)
        carry = back_block(last, carry, odd_g_s, odd_p_s)
        read_grads(last, odd_g_s, odd_p_s)
        return back_block(last - 1, carry, even_g_s, even_p_s)

    lax.fori_loop(0, blocks // 2, backward, jnp.zeros((state_dim, width), f32))
    read_grads(0, even_g_s, even_p_s)
    gq_s[...] += gqt_s[...]
    ge_s[...] += get_s[...]
    pe_s[...] += pet_s[...]

    xs = xs_ref[...].astype(f32)
    z = z_ref[...]
    skip = skip_ref[...].astype(f32)
    sig = jax.nn.sigmoid(z)
    mixed = y_s[...] + skip * xs
    gated = (mixed * (z * sig)).astype(bf16)
    gated_ref[...] = gated
    out_part = jnp.dot(gated, wo_ref[...], preferred_element_type=f32)
    gz_ref[...] = (gg_s[...] * mixed * (sig * (1.0 + z * (1.0 - sig)))).astype(bf16)
    gm = gm_s[...]
    s1 = s1_s[...]
    eps = eps_s[...]
    g_eps = xs * s1 - s2_s[...]
    sum_s[...] += jnp.broadcast_to(jnp.sum(g_eps * eps * eps, axis=1, keepdims=True), sum_s.shape)
    g_dt = (g_eps * slope_s[...]).astype(bf16)
    dtg_ref[...] = mm(low, g_dt, (1, 0))
    gxs_ref[...] = skip * gm + eps * s1
    small_ref[0:1, :] = jnp.sum(gm * xs, axis=0, keepdims=True)
    small_ref[1:2, :] = jnp.sum(g_dt.astype(f32), axis=0, keepdims=True)
    small_ref[2:, :] = jnp.zeros((6, width), f32)
    g_low = mm(wdt_ref[...], g_dt, (1, 1))

    @pl.when(step == 0)
    def _():
        gproj_s[...] = g_low
        acc_s[...] = out_part

    @pl.when(step > 0)
    def _():
        gproj_s[...] += g_low
        acc_s[...] += out_part

    @pl.when(step == pl.num_programs(0) - 1)
    def _():
        scale = sum_s[...].T[0:1, :]
        for b in range(blocks):
            cols = slice(b * BLOCK, (b + 1) * BLOCK)
            own_keys = ge_s[b, :, :BLOCK] - 2.0 * kt_s[b, :, :BLOCK] * (pe_s[b, :, :BLOCK] + scale[:, cols])
            tail_s[:state_dim, cols] = own_keys
            tail_s[state_dim:, cols] = gq_s[b, :, :BLOCK]
        gproj_ref[:rank, :] = gproj_s[...].astype(bf16)
        gproj_ref[rank:, :] = tail_s[...].astype(bf16)
        out_ref[...] = acc_s[...].astype(bf16)


def recurrence(keep, offs, parts, terms, xs, z, wo, wdt, dt_bias, skip):
    seq_len, inner = xs.shape
    model = wo.shape[1]
    rank = wdt.shape[0]
    columns = terms[0].shape[0]
    state_dim = (columns - rank) // 2
    wide = 512
    flat = BLOCK * state_dim
    blocks = seq_len // BLOCK
    vmem = pltpu.VMEM
    return pl.pallas_call(
        functools.partial(recurrence_kernel, state_dim, rank, len(parts)),
        grid=(inner // wide,),
        in_specs=[pl.BlockSpec(memory_space=pltpu.SMEM)] * 2
        + [whole_of(parts[0].shape)] * len(parts)
        + [whole_of((columns, seq_len))] * len(terms)
        + [
            blocks_of(seq_len, wide),
            blocks_of(seq_len, wide),
            pl.BlockSpec((wide, model), lambda c: (c, 0)),
            blocks_of(rank, wide),
            blocks_of(1, wide),
            blocks_of(1, wide),
        ],
        out_specs=[
            blocks_of(seq_len, wide),
            blocks_of(seq_len, wide),
            blocks_of(seq_len, wide),
            whole_of((columns, seq_len)),
            blocks_of(8, wide),
            blocks_of(rank, wide),
            whole_of((seq_len, model)),
            whole_of((seq_len, model)),
        ],
        out_shape=[
            jax.ShapeDtypeStruct((seq_len, inner), bf16),
            jax.ShapeDtypeStruct((seq_len, inner), bf16),
            jax.ShapeDtypeStruct((seq_len, inner), f32),
            jax.ShapeDtypeStruct((columns, seq_len), bf16),
            jax.ShapeDtypeStruct((8, inner), f32),
            jax.ShapeDtypeStruct((rank, inner), f32),
            jax.ShapeDtypeStruct((seq_len, model), bf16),
            jax.ShapeDtypeStruct((seq_len, model), bf16),
        ],
        scratch_shapes=[
            vmem((seq_len, wide), f32),
            vmem((columns, seq_len), f32),
            vmem((rank, seq_len), f32),
            vmem((seq_len, model), f32),
            vmem((seq_len, wide), f32),
        ]
        + [vmem((seq_len, wide), f32)] * 6
        + [vmem(((seq_len + 1) * state_dim, wide), bf16)]
        + [vmem((flat, wide), bf16)] * 4
        + [vmem((blocks, state_dim, LANES), f32)] * 2
        + [vmem((seq_len, flat), bf16)] * 3
        + [vmem((seq_len, LANES), f32)] * 2
        + [vmem((2 * state_dim, seq_len), f32)]
        + [vmem((blocks, state_dim, LANES), f32)] * 6,
        name="recurrence",
        cost_estimate=pl.CostEstimate(
            flops=60 * seq_len * state_dim * inner + 4 * seq_len * model * inner,
            bytes_accessed=2 * model * inner + 20 * seq_len * inner,
            transcendentals=6 * seq_len * inner,
        ),
    )(keep, offs, *parts, *terms, xs, z, wo, wdt, dt_bias, skip)


def grad_kernel(place_ref, la_ref, lb_ref, ra_ref, rb_ref, out_ref):
    out_ref[0] = (mm(la_ref[...], ra_ref[...], (0, 0)) + mm(lb_ref[...], rb_ref[...], (0, 0))).astype(bf16)


def grad_add_kernel(place_ref, la_ref, lb_ref, ra_ref, rb_ref, got_ref, out_ref):
    total = mm(la_ref[...], ra_ref[...], (0, 0)) + mm(lb_ref[...], rb_ref[...], (0, 0))
    out_ref[0] = (total + got_ref[0].astype(f32)).astype(bf16)


def grad_slices(left, right, own, parts, got=None):
    seq_len, model = left[0].shape
    inner = right[0].shape[1]
    rows = model // parts
    if rows % LANES:
        total = sum(mm(a, b, (0, 0)) for a, b in zip(left, right)).reshape(parts // 2, 2, rows, inner)
        total = take_bit(total, 1, own)
        return (total if got is None else total + got.astype(f32)).astype(bf16)
    place = own.reshape(1).astype(jnp.int32)
    lhs = pl.BlockSpec((seq_len, rows), lambda j, place: (0, 2 * j + place[0]))
    rhs = pl.BlockSpec((seq_len, inner), lambda j, place: (0, 0))
    block = pl.BlockSpec((1, rows, inner), lambda j, place: (j, 0, 0))
    kernel = grad_kernel if got is None else grad_add_kernel
    extra = () if got is None else (got,)
    return pl.pallas_call(
        kernel,
        grid_spec=pltpu.PrefetchScalarGridSpec(
            num_scalar_prefetch=1,
            grid=(parts // 2,),
            in_specs=[lhs, lhs, rhs, rhs] + [block] * len(extra),
            out_specs=block,
        ),
        out_shape=jax.ShapeDtypeStruct((parts // 2, rows, inner), bf16),
        name="weight_grad",
        cost_estimate=pl.CostEstimate(
            flops=2 * seq_len * model * inner,
            bytes_accessed=2 * seq_len * (model + 2 * inner) + 2 * model * inner,
            transcendentals=0,
        ),
    )(place, *left, *right, *extra)


def after(x, *others):
    return lax.optimization_barrier((x, others))[0]


def per_device(
    states_in,
    out_cotangent,
    segments,
    starts,
    norm_gain,
    in_x_weight,
    in_z_weight,
    conv_weight,
    conv_bias,
    x_proj_weight,
    dt_weight,
    dt_bias,
    skip_weight,
    out_weight,
):
    count, rows, model = states_in.shape
    span, inner = conv_weight.shape
    rank = dt_weight.shape[0]
    seq_len = segments.shape[1]
    dp = lax.axis_size("dp")
    gain = norm_gain.astype(f32)
    proj_weight = x_proj_weight.T
    keep = 1.0 - starts[:, ::8].astype(f32)
    seqs = range(count)
    me = lax.axis_index("fsdp")
    core = lax.rem(lax.axis_index("dp"), 2)
    offs = jnp.stack([(me ^ mask) * rows for mask in range(lax.axis_size("fsdp"))])[None, :].astype(jnp.int32)
    tap_bias = conv_bias[None, :]
    normed, xin, xs, z, masks, projs = [], [], [], [], [], []
    gated, gz, gxs, gprojs, small, dtg, cots, branch = [], [], [], [], [], [], [], []
    g_x_in, gn, rows_part, proj_part, gain_part = [], [], [], [], []
    tokens, cot_parts = [], []
    behind = ()
    for s in seqs:
        for source, into in ((states_in, tokens), (out_cotangent, cot_parts)):
            into.append(gather_parts(after(source[s], *behind), "fsdp"))
            behind = (into[s][-2],)
    for s in seqs:
        seg_ext = jnp.pad(segments[s], (span - 1, 0), constant_values=-1)
        mask = jnp.stack([(seg_ext[w : w + seq_len] == segments[s]).astype(f32) for w in range(span)], 1)
        masks.append(jnp.pad(mask, ((0, 0), (0, LANES - span))))

    def run_enter(s):
        got = enter(
            offs, tokens[s], norm_gain[None, :], masks[s], in_x_weight, in_z_weight, conv_weight, tap_bias, proj_weight
        )
        for into, value in zip((normed, xin, z, xs), got):
            into.append(value)
        projs.append(exchange_all(got[4], "fsdp"))

    def run_recurrence(s):
        got = recurrence(
            keep[s : s + 1],
            offs,
            cot_parts[s],
            projs[s],
            xs[s],
            z[s],
            out_weight,
            dt_weight,
            dt_bias[None, :],
            skip_weight[None, :],
        )
        for into, value in zip((gated, gz, gxs, gprojs, small, dtg, cots, branch), got):
            into.append(value)
        gprojs[s] = exchange_all(gprojs[s], "fsdp")
        branch[s] = scatter_of(branch[s], "fsdp")

    def run_leave(s, *behind):
        got = leave(
            gprojs[s],
            proj_weight,
            after(gxs[s], *behind),
            xin[s],
            xs[s],
            gz[s],
            masks[s],
            conv_weight,
            tap_bias,
            in_x_weight,
            in_z_weight,
            normed[s],
        )
        for into, value in zip((g_x_in, gn, rows_part, proj_part, gain_part), got):
            into.append(value)
        gn[s] = scatter_of(gn[s], "fsdp")

    run_enter(0)
    run_enter(1)
    run_recurrence(0)
    run_recurrence(1)
    first_a = branch[0].send()
    out_sent = swap(grad_slices(cots, [gated[0], after(gated[1], first_a)], 1 - core, dp), "dp", 1)
    z_sent = swap(grad_slices(normed, gz, 1 - core, dp), "dp", 1)
    branch[0].add()
    out_parts = scatter_rest(grad_slices(cots, gated, core, dp, out_sent))
    z_parts = scatter_rest(grad_slices(normed, gz, core, dp, z_sent))
    started = [part.send() for part in out_parts + z_parts]
    second_a = branch[0].send()
    run_leave(0, out_parts[0].x, z_parts[0].x)
    for part in out_parts:
        part.add()
        part.send()
    first_b = branch[1].send()
    first_gn = gn[0].send()
    run_leave(1, second_a, started[0], started[1], gn[0].x)
    for part in z_parts:
        part.add()
        part.send()
    gn[0].add()
    second_gn = gn[0].send()
    later = (started[2], started[3], out_parts[0].got, out_parts[1].got, first_gn, first_b)
    x_sent = swap(grad_slices(normed, [g_x_in[0], after(g_x_in[1], *later)], 1 - core, dp), "dp", 1)
    gn[1].send()
    x_parts = scatter_rest(grad_slices(normed, g_x_in, core, dp, x_sent))

    def join(parts):
        return jnp.concatenate([part.finish() for part in parts], 0)

    def end(scatter):
        if scatter.left:
            scatter.add()
        return scatter.finish()

    out_grad = jnp.concatenate([end(part) for part in out_parts], 0).T
    in_z_grad = jnp.concatenate([end(part) for part in z_parts], 0)
    in_x_grad = join(x_parts)
    outputs, input_grads = [], []
    for s in seqs:
        outputs.append((states_in[s].astype(f32) + end(branch[s])).astype(bf16))
        v = states_in[s].astype(f32)
        rscale = lax.rsqrt(jnp.mean(v * v, axis=1, keepdims=True) + norm_eps)
        scaled = end(gn[s]) * gain
        inner_mean = jnp.mean(scaled * v, axis=1, keepdims=True)
        input_grads.append(out_cotangent[s].astype(f32) + rscale * scaled - v * (rscale * rscale * rscale) * inner_mean)

    dt_grad = scatter_of(sum(dtg), "dp").finish()
    rows_sum = jnp.concatenate([sum(rows_part)[: span + 1], sum(small)[1::-1]], 0)
    packed = all_sum(jnp.concatenate([rows_sum, sum(proj_part), jnp.zeros((1, inner), f32)], 0), "dp")
    gain_grad = all_sum(all_sum(sum(gain_part)[0], "fsdp", f32), "dp", f32) / gain
    first = span + 3
    return (
        jnp.stack(outputs),
        jnp.stack(input_grads),
        gain_grad,
        in_x_grad,
        in_z_grad,
        packed[:span],
        packed[span],
        packed[first : first + proj_weight.shape[0]].T,
        dt_grad,
        packed[span + 1],
        packed[span + 2],
        out_grad,
    )


def solution(mesh):
    in_specs = (
        P("dp", "fsdp", None),
        P("dp", "fsdp", None),
        P("dp", None),
        P("dp", None),
        P(),
        P(None, "fsdp"),
        P(None, "fsdp"),
        P(None, "fsdp"),
        P("fsdp"),
        P("fsdp", None),
        P(None, "fsdp"),
        P("fsdp"),
        P("fsdp"),
        P("fsdp", None),
    )
    out_specs = (
        P("dp", "fsdp", None),
        P("dp", "fsdp", None),
        P(),
        P("dp", "fsdp"),
        P("dp", "fsdp"),
        P(None, "fsdp"),
        P("fsdp"),
        P("fsdp", None),
        P("dp", "fsdp"),
        P("fsdp"),
        P("fsdp"),
        P("fsdp", "dp"),
    )
    return jax.shard_map(per_device, mesh=mesh, in_specs=in_specs, out_specs=out_specs, check_vma=False)
```

```python
import functools

import jax
import jax.numpy as jnp
from jax import lax
from jax.experimental import pallas as pl
from jax.experimental.pallas import tpu as pltpu
from jax.sharding import PartitionSpec as P

BLOCK = 16
LANES = 128
norm_eps = 1e-05


def takes(microseconds):
    return pl.CostEstimate(flops=int(microseconds * 9e8), bytes_accessed=1, transcendentals=0)
f32 = jnp.float32
bf16 = jnp.bfloat16


def mm(left, right, contract):
    return lax.dot_general(left, right, ((contract[:1], contract[1:]), ((), ())), preferred_element_type=f32)


def swap(x, axis, bit):
    return lax.ppermute(x, axis, [(i, i ^ bit) for i in range(lax.axis_size(axis))])


def bits_of(count):
    return [1 << k for k in range(count.bit_length() - 1)]


def exchange_all(x, axis):
    return [x] + [swap(x, axis, mask) for mask in range(1, lax.axis_size(axis))]


def relay_all(x, axis):
    held = {0: x}
    for bit in reversed(bits_of(lax.axis_size(axis))):
        for mask in list(held):
            held[mask | bit] = swap(held[mask], axis, bit)
    return [held[mask] for mask in range(len(held))]


class RowScatter:
    def __init__(self, sent, kept, axis):
        self.axis, self.bits = axis, bits_of(lax.axis_size(axis))
        self.sent, self.kept = sent, kept

    def send(self, *behind):
        self.got = swap(after(self.sent, *behind), self.axis, self.bits.pop(0))

    def mid(self):
        self.sent = (self.kept[1::2].astype(f32) + self.got[1::2].astype(f32)).astype(bf16)
        self.kept = (self.kept[0::2].astype(f32) + self.got[0::2].astype(f32))

    def finish(self):
        while self.bits:
            self.mid()
            self.send()
        return self.kept[0].astype(f32) + self.got[0].astype(f32)


def after(x, *others):
    return lax.optimization_barrier((x, others))[0] if others else x


def sum_pair(x, axis):
    bits = bits_of(lax.axis_size(axis))
    for bit in bits[:-1]:
        x = (x.astype(f32) + swap(x, axis, bit).astype(f32)).astype(bf16)
    return [x, swap(x, axis, bits[-1])]


def take_bit(x, dim, value):
    return lax.dynamic_index_in_dim(x, value, dim, keepdims=False)


class Scatter:
    def __init__(self, x, axis, bits, dims):
        self.x, self.axis, self.left = x, axis, list(zip(bits, dims))

    def send(self):
        bit, dim = self.left[0]
        own = (lax.axis_index(self.axis) // bit) % 2
        self.got = swap(take_bit(self.x, dim, 1 - own).astype(bf16), self.axis, bit)
        self.kept = take_bit(self.x, dim, own)
        return self.got

    def add(self):
        _, dim = self.left.pop(0)
        self.left = [(bit, d - 1 if d > dim else d) for bit, d in self.left]
        self.x = self.kept.astype(f32) + self.got.astype(f32)

    def finish(self):
        while self.left:
            self.send()
            self.add()
        return self.x


def scatter_of(x, axis):
    count = lax.axis_size(axis)
    bits = bits_of(count)
    n = len(bits)
    return Scatter(x.reshape((2,) * n + (x.shape[0] // count,) + x.shape[1:]), axis, bits, range(n - 1, -1, -1))


def all_sum(x, axis, kind=bf16):
    for bit in bits_of(lax.axis_size(axis)):
        low = x.astype(kind)
        x = low.astype(f32) + swap(low, axis, bit).astype(f32)
    return x


def far(x):
    return pltpu.with_memory_space_constraint(x, pltpu.HBM)


def add_up(refs):
    total = refs[0][...].astype(f32)
    for ref in refs[1:]:
        total = total + ref[...].astype(f32)
    return total


def silu_slope(v):
    s = jax.nn.sigmoid(v)
    return s * (1.0 + v * (1.0 - s))


def conv_sum(x, masks, taps, bias):
    span = taps.shape[0]
    total = bias + taps[span - 1 : span] * x
    shifted = []
    for w in range(span - 1):
        moved = pltpu.roll(x, span - 1 - w, 0) * masks[:, w : w + 1]
        shifted.append(moved)
        total = total + taps[w : w + 1] * moved
    return total, shifted + [x]


def enter_kernel(count, offs_ref, *refs):
    parts = refs[:count]
    gain_ref, mask_ref, wx_ref, wz_ref, taps_ref, bias_ref, wp_ref = refs[count : count + 7]
    normed_ref, xin_ref, z_ref, xs_ref, proj_ref, acc_s = refs[count + 7 :]
    step = pl.program_id(0)

    @pl.when(step == 0)
    def _():
        gain = gain_ref[...].astype(f32)
        for m, part in enumerate(parts):
            v = part[...].astype(f32)
            rscale = lax.rsqrt(jnp.mean(v * v, axis=1, keepdims=True) + norm_eps)
            rows = part.shape[0]
            normed_ref[pl.ds(pl.multiple_of(offs_ref[0, m], rows), rows), :] = (v * rscale * gain).astype(bf16)
        acc_s[...] = jnp.zeros_like(acc_s)

    normed = normed_ref[...]
    z_ref[...] = jnp.dot(normed, wz_ref[...], preferred_element_type=f32)
    x_in = jnp.dot(normed, wx_ref[...], preferred_element_type=f32).astype(bf16)
    xin_ref[...] = x_in
    pre, _ = conv_sum(x_in.astype(f32), mask_ref[...], taps_ref[...].astype(f32), bias_ref[...].astype(f32))
    xs = jax.nn.silu(pre).astype(bf16)
    xs_ref[...] = xs
    acc_s[...] += mm(wp_ref[...], xs, (1, 1))

    @pl.when(step == pl.num_programs(0) - 1)
    def _():
        proj_ref[...] = acc_s[...].astype(bf16)


def blocks_of(rows, wide):
    return pl.BlockSpec((rows, wide), lambda c: (0, c))


def whole_of(shape):
    return pl.BlockSpec(shape, lambda c: (0,) * len(shape))


def enter(offs, parts, gain, masks, wx, wz, taps, bias, wp):
    rows, model = parts[0].shape
    seq_len = rows * len(parts)
    inner = wx.shape[1]
    wide = 256
    return pl.pallas_call(
        functools.partial(enter_kernel, len(parts)),
        grid=(inner // wide,),
        in_specs=[pl.BlockSpec(memory_space=pltpu.SMEM)]
        + [whole_of((rows, model))] * len(parts)
        + [
            whole_of((1, model)),
            whole_of(masks.shape),
            blocks_of(model, wide),
            blocks_of(model, wide),
            blocks_of(taps.shape[0], wide),
            blocks_of(1, wide),
            blocks_of(wp.shape[0], wide),
        ],
        out_specs=[
            whole_of((seq_len, model)),
            blocks_of(seq_len, wide),
            blocks_of(seq_len, wide),
            blocks_of(seq_len, wide),
            whole_of((wp.shape[0], seq_len)),
        ],
        out_shape=[
            jax.ShapeDtypeStruct((seq_len, model), bf16),
            jax.ShapeDtypeStruct((seq_len, inner), bf16),
            jax.ShapeDtypeStruct((seq_len, inner), f32),
            jax.ShapeDtypeStruct((seq_len, inner), bf16),
            jax.ShapeDtypeStruct((wp.shape[0], seq_len), bf16),
        ],
        scratch_shapes=[pltpu.VMEM((wp.shape[0], seq_len), f32)],
        name="enter",
        compiler_params=pltpu.CompilerParams(vmem_limit_bytes=20 * 1024 * 1024),
        cost_estimate=takes(9),
    )(offs, *parts, gain, masks, wx, wz, taps, bias, wp)


def write_parts(offs_ref, total_s, sent_ref, kept_ref):
    count, rows = kept_ref.shape[0], kept_ref.shape[1]
    for m in range(count):
        for odd, out in ((0, kept_ref), (1, sent_ref)):
            off = pl.multiple_of(offs_ref[0, 2 * m + odd], rows)
            out[m] = total_s[pl.ds(off, rows), :].astype(bf16)


def leave_kernel(count, offs_ref, *refs):
    terms = refs[:count]
    wp_ref, gxs_ref, xin_ref, xs_ref, gz_ref, mask_ref, taps_ref, bias_ref, wx_ref, wz_ref, normed_ref = refs[
        count : count + 11
    ]
    gxin_ref, rows_ref, xpg_ref, gain_ref = refs[count + 11 : count + 15]
    sent_ref, kept_ref, acc_s = refs[count + 15 :]
    step = pl.program_id(0)
    span = taps_ref.shape[0]
    seq_len = xin_ref.shape[0]
    gproj = add_up(terms).astype(bf16)
    xpg_ref[...] = mm(gproj, xs_ref[...], (1, 0))
    g_xs = gxs_ref[...] + mm(gproj, wp_ref[...], (0, 0))
    masks = mask_ref[...]
    taps = taps_ref[...].astype(f32)
    pre, shifted = conv_sum(xin_ref[...].astype(f32), masks, taps, bias_ref[...].astype(f32))
    g_conv = g_xs * silu_slope(pre)
    total = taps[span - 1 : span] * g_conv
    for w in range(span):
        rows_ref[w : w + 1, :] = jnp.sum(g_conv * shifted[w], axis=0, keepdims=True)
        if w < span - 1:
            term = g_conv * masks[:, w : w + 1] * taps[w : w + 1]
            total = total + pltpu.roll(term, seq_len - (span - 1 - w), 0)
    rows_ref[span : span + 1, :] = jnp.sum(g_conv, axis=0, keepdims=True)
    rows_ref[span + 1 :, :] = jnp.zeros((8 - span - 1, g_conv.shape[1]), f32)
    g_x_in = total.astype(bf16)
    gxin_ref[...] = g_x_in
    gn = mm(g_x_in, wx_ref[...], (1, 1)) + mm(gz_ref[...], wz_ref[...], (1, 1))

    @pl.when(step == 0)
    def _():
        acc_s[...] = gn

    @pl.when(step > 0)
    def _():
        acc_s[...] += gn

    @pl.when(step == pl.num_programs(0) - 1)
    def _():
        gn = acc_s[...]
        write_parts(offs_ref, acc_s, sent_ref, kept_ref)
        gain_ref[...] = jnp.sum(gn * normed_ref[...].astype(f32), axis=0, keepdims=True)


def leave(offs, terms, wp, gxs, xin, xs, gz, masks, taps, bias, wx, wz, normed):
    seq_len, model = normed.shape
    inner = wx.shape[1]
    count = offs.shape[1]
    wide = 256
    return pl.pallas_call(
        functools.partial(leave_kernel, len(terms)),
        grid=(inner // wide,),
        in_specs=[pl.BlockSpec(memory_space=pltpu.SMEM)]
        + [whole_of(terms[0].shape)] * len(terms)
        + [
            blocks_of(wp.shape[0], wide),
            blocks_of(seq_len, wide),
            blocks_of(seq_len, wide),
            blocks_of(seq_len, wide),
            blocks_of(seq_len, wide),
            whole_of(masks.shape),
            blocks_of(taps.shape[0], wide),
            blocks_of(1, wide),
            blocks_of(model, wide),
            blocks_of(model, wide),
            whole_of((seq_len, model)),
        ],
        out_specs=[
            blocks_of(seq_len, wide),
            blocks_of(8, wide),
            blocks_of(wp.shape[0], wide),
            whole_of((1, model)),
        ]
        + [whole_of((count // 2, seq_len // count, model))] * 2,
        out_shape=[
            jax.ShapeDtypeStruct((seq_len, inner), bf16),
            jax.ShapeDtypeStruct((8, inner), f32),
            jax.ShapeDtypeStruct((wp.shape[0], inner), f32),
            jax.ShapeDtypeStruct((1, model), f32),
        ]
        + [jax.ShapeDtypeStruct((count // 2, seq_len // count, model), bf16)] * 2,
        scratch_shapes=[pltpu.VMEM((seq_len, model), f32)],
        name="leave",
        compiler_params=pltpu.CompilerParams(vmem_limit_bytes=24 * 1024 * 1024),
        cost_estimate=takes(10),
    )(offs, *terms, wp, gxs, xin, xs, gz, masks, taps, bias, wx, wz, normed)


def recurrence_kernel(state_dim, rank, count, keep_ref, offs_ref, *refs):
    parts, terms, refs = refs[:count], refs[count : count + 2], refs[count + 2 :]
    xs_ref, z_ref, wo_ref, wdt_ref, dtb_ref, skip_ref = refs[:6]
    gated_ref, gz_ref, gxs_ref, gproj_ref, small_ref, dtg_ref, cot_ref, sent_ref, kept_ref = refs[6:15]
    (
        gg_s,
        proj_s,
        gproj_s,
        acc_s,
        slope_s,
        eps_s,
        u_s,
        gm_s,
        y_s,
        s1_s,
        s2_s,
        hist_s,
        even_g_s,
        odd_g_s,
        even_p_s,
        odd_p_s,
        kt_s,
        qt_s,
        kd_s,
        k2d_s,
        qd_s,
        norm_s,
        sum_s,
        tail_s,
        gq_s,
        ge_s,
        pe_s,
        gqt_s,
        get_s,
        pet_s,
    ) = refs[15:]
    step = pl.program_id(0)
    seq_len, width = xs_ref.shape
    blocks = seq_len // BLOCK
    flat = BLOCK * state_dim
    lane = lax.broadcasted_iota(jnp.int32, (state_dim, BLOCK), 1)

    @pl.when(step == 0)
    def _():
        proj_s[...] = add_up(terms)
        for m, part in enumerate(parts):
            rows = part.shape[0]
            cot_ref[pl.ds(pl.multiple_of(offs_ref[0, m], rows), rows), :] = part[...]
        turned = proj_s[rank:, :]
        for b in range(blocks):
            cols = slice(b * BLOCK, (b + 1) * BLOCK)
            kt_s[b] = jnp.pad(turned[:state_dim, cols], ((0, 0), (0, LANES - BLOCK)))
            qt_s[b] = jnp.pad(turned[state_dim:, cols], ((0, 0), (0, LANES - BLOCK)))
        source = lax.broadcasted_iota(jnp.int32, (2 * state_dim, flat), 0)
        target = lax.rem(lax.broadcasted_iota(jnp.int32, (2 * state_dim, flat), 1), state_dim)
        take_k = (source == target).astype(bf16)
        take_q = (source == target + state_dim).astype(bf16)
        own = (
            lax.rem(lax.broadcasted_iota(jnp.int32, (seq_len, flat), 0), BLOCK)
            == lax.broadcasted_iota(jnp.int32, (seq_len, flat), 1) // state_dim
        )
        kd_s[...] = jnp.where(own, mm(turned.astype(bf16), take_k, (0, 0)), 0.0).astype(bf16)
        k2d_s[...] = jnp.where(own, mm((turned * turned).astype(bf16), take_k, (0, 0)), 0.0).astype(bf16)
        qd_s[...] = jnp.where(own, mm(turned.astype(bf16), take_q, (0, 0)), 0.0).astype(bf16)
        square = jnp.sum(turned[:state_dim] * turned[:state_dim], axis=0, keepdims=True)
        norm_s[...] = jnp.broadcast_to(square, (LANES, seq_len)).T
        sum_s[...] = jnp.zeros_like(sum_s)
        gq_s[...] = jnp.zeros_like(gq_s)
        ge_s[...] = jnp.zeros_like(ge_s)
        pe_s[...] = jnp.zeros_like(pe_s)

    gg_s[...] = mm(cot_ref[...], wo_ref[...], (1, 1))
    low = proj_s[:rank, :].astype(bf16)
    dt_pre = mm(low, wdt_ref[...], (0, 0)) + dtb_ref[...].astype(f32)
    rates = jnp.maximum(dt_pre, 0.0) + jnp.log1p(jnp.exp(-jnp.abs(dt_pre)))
    ratio = 1.0 / (1.0 + rates * norm_s[:, 0:1])
    eps_s[...] = rates * ratio
    slope_s[...] = ratio * ratio * jax.nn.sigmoid(dt_pre)
    u_s[...] = eps_s[...] * xs_ref[...].astype(f32)
    gm_s[...] = gg_s[...] * jax.nn.silu(z_ref[...])
    hist_s[0:state_dim, :] = jnp.zeros((state_dim, width), bf16)

    def own_token(pairs):
        picked = pairs[:state_dim]
        for t in range(1, BLOCK):
            picked = jnp.where(lane == t, pairs[t * state_dim : (t + 1) * state_dim], picked)
        return picked

    def read_states(b, buf):
        toks = pl.ds(pl.multiple_of(b * BLOCK, BLOCK), BLOCK)
        hblk = buf[...]
        y_s[toks, :] = jnp.dot(qd_s[toks, :], hblk, preferred_element_type=f32)
        gqt_s[b, :, :BLOCK] = own_token(mm(hblk, gm_s[toks, :].astype(bf16), (1, 1)))

    def scan_block(b, h, buf):
        base = pl.multiple_of(b * BLOCK, BLOCK)
        kt = kt_s[b]
        for t in range(BLOCK):
            if t % 8 == 0:
                h = h * keep_ref[0, b * 2 + t // 8]
            col = jnp.broadcast_to(kt[:, t : t + 1], (state_dim, width))
            e = eps_s[pl.ds(base + t, 1), :]
            u = u_s[pl.ds(base + t, 1), :]
            h = (1.0 - (col * col) * e) * h + col * u
            kept = h.astype(bf16)
            hist_s[pl.ds(pl.multiple_of((base + t + 1) * state_dim, state_dim), state_dim), :] = kept
            buf[t * state_dim : (t + 1) * state_dim, :] = kept
        return h

    def forward(i, h):
        read_states(jnp.maximum(2 * i - 1, 0), odd_g_s)
        h = scan_block(2 * i, h, even_g_s)
        read_states(2 * i, even_g_s)
        return scan_block(2 * i + 1, h, odd_g_s)

    lax.fori_loop(0, blocks // 2, forward, jnp.zeros((state_dim, width), f32))
    read_states(blocks - 1, odd_g_s)

    def read_grads(b, gbuf, pbuf):
        toks = pl.ds(pl.multiple_of(b * BLOCK, BLOCK), BLOCK)
        gblk = gbuf[...]
        pblk = pbuf[...]
        s1_s[toks, :] = jnp.dot(kd_s[toks, :], gblk, preferred_element_type=f32)
        s2_s[toks, :] = jnp.dot(k2d_s[toks, :], pblk, preferred_element_type=f32)
        get_s[b, :, :BLOCK] = own_token(mm(gblk, u_s[toks, :].astype(bf16), (1, 1)))
        pet_s[b, :, :BLOCK] = own_token(mm(pblk, eps_s[toks, :].astype(bf16), (1, 1)))

    def back_block(b, carry, gbuf, pbuf):
        base = pl.multiple_of(b * BLOCK, BLOCK)
        kt = kt_s[b]
        qt = qt_s[b]
        for t in reversed(range(BLOCK)):
            colq = jnp.broadcast_to(qt[:, t : t + 1], (state_dim, width))
            col = jnp.broadcast_to(kt[:, t : t + 1], (state_dim, width))
            e = eps_s[pl.ds(base + t, 1), :]
            gm = gm_s[pl.ds(base + t, 1), :]
            g = colq * gm + carry
            before = hist_s[pl.ds(pl.multiple_of((base + t) * state_dim, state_dim), state_dim), :].astype(f32)
            p = g * before
            carry = (1.0 - (col * col) * e) * g
            if t % 8 == 0:
                k = keep_ref[0, b * 2 + t // 8]
                carry = carry * k
                p = p * k
            gbuf[t * state_dim : (t + 1) * state_dim, :] = g.astype(bf16)
            pbuf[t * state_dim : (t + 1) * state_dim, :] = p.astype(bf16)
        return carry

    def backward(i, carry):
        last = blocks - 1 - 2 * i
        read_grads(jnp.minimum(last + 1, blocks - 1), even_g_s, even_p_s)
        carry = back_block(last, carry, odd_g_s, odd_p_s)
        read_grads(last, odd_g_s, odd_p_s)
        return back_block(last - 1, carry, even_g_s, even_p_s)

    lax.fori_loop(0, blocks // 2, backward, jnp.zeros((state_dim, width), f32))
    read_grads(0, even_g_s, even_p_s)
    gq_s[...] += gqt_s[...]
    ge_s[...] += get_s[...]
    pe_s[...] += pet_s[...]

    xs = xs_ref[...].astype(f32)
    z = z_ref[...]
    skip = skip_ref[...].astype(f32)
    sig = jax.nn.sigmoid(z)
    mixed = y_s[...] + skip * xs
    gated = (mixed * (z * sig)).astype(bf16)
    gated_ref[...] = gated
    out_part = jnp.dot(gated, wo_ref[...], preferred_element_type=f32)
    gz_ref[...] = (gg_s[...] * mixed * (sig * (1.0 + z * (1.0 - sig)))).astype(bf16)
    gm = gm_s[...]
    s1 = s1_s[...]
    eps = eps_s[...]
    g_eps = xs * s1 - s2_s[...]
    sum_s[...] += jnp.broadcast_to(jnp.sum(g_eps * eps * eps, axis=1, keepdims=True), sum_s.shape)
    g_dt = (g_eps * slope_s[...]).astype(bf16)
    dtg_ref[...] = mm(low, g_dt, (1, 0))
    gxs_ref[...] = skip * gm + eps * s1
    small_ref[0:1, :] = jnp.sum(gm * xs, axis=0, keepdims=True)
    small_ref[1:2, :] = jnp.sum(g_dt.astype(f32), axis=0, keepdims=True)
    small_ref[2:, :] = jnp.zeros((6, width), f32)
    g_low = mm(wdt_ref[...], g_dt, (1, 1))

    @pl.when(step == 0)
    def _():
        gproj_s[...] = g_low
        acc_s[...] = out_part

    @pl.when(step > 0)
    def _():
        gproj_s[...] += g_low
        acc_s[...] += out_part

    @pl.when(step == pl.num_programs(0) - 1)
    def _():
        scale = sum_s[...].T[0:1, :]
        for b in range(blocks):
            cols = slice(b * BLOCK, (b + 1) * BLOCK)
            own_keys = ge_s[b, :, :BLOCK] - 2.0 * kt_s[b, :, :BLOCK] * (pe_s[b, :, :BLOCK] + scale[:, cols])
            tail_s[:state_dim, cols] = own_keys
            tail_s[state_dim:, cols] = gq_s[b, :, :BLOCK]
        gproj_ref[:rank, :] = gproj_s[...].astype(bf16)
        gproj_ref[rank:, :] = tail_s[...].astype(bf16)
        write_parts(offs_ref, acc_s, sent_ref, kept_ref)


def recurrence(keep, offs, parts, terms, xs, z, wo, wdt, dt_bias, skip):
    seq_len, inner = xs.shape
    model = wo.shape[1]
    rank = wdt.shape[0]
    columns = terms[0].shape[0]
    state_dim = (columns - rank) // 2
    wide = 512
    flat = BLOCK * state_dim
    blocks = seq_len // BLOCK
    vmem = pltpu.VMEM
    return pl.pallas_call(
        functools.partial(recurrence_kernel, state_dim, rank, len(parts)),
        grid=(inner // wide,),
        in_specs=[pl.BlockSpec(memory_space=pltpu.SMEM)] * 2
        + [whole_of(parts[0].shape)] * len(parts)
        + [whole_of((columns, seq_len))] * len(terms)
        + [
            blocks_of(seq_len, wide),
            blocks_of(seq_len, wide),
            pl.BlockSpec((wide, model), lambda c: (c, 0)),
            blocks_of(rank, wide),
            blocks_of(1, wide),
            blocks_of(1, wide),
        ],
        out_specs=[
            blocks_of(seq_len, wide),
            blocks_of(seq_len, wide),
            blocks_of(seq_len, wide),
            whole_of((columns, seq_len)),
            blocks_of(8, wide),
            blocks_of(rank, wide),
            whole_of((seq_len, model)),
        ]
        + [whole_of((len(parts) // 2,) + parts[0].shape)] * 2,
        out_shape=[
            jax.ShapeDtypeStruct((seq_len, inner), bf16),
            jax.ShapeDtypeStruct((seq_len, inner), bf16),
            jax.ShapeDtypeStruct((seq_len, inner), f32),
            jax.ShapeDtypeStruct((columns, seq_len), bf16),
            jax.ShapeDtypeStruct((8, inner), f32),
            jax.ShapeDtypeStruct((rank, inner), f32),
            jax.ShapeDtypeStruct((seq_len, model), bf16),
        ]
        + [jax.ShapeDtypeStruct((len(parts) // 2,) + parts[0].shape, bf16)] * 2,
        scratch_shapes=[
            vmem((seq_len, wide), f32),
            vmem((columns, seq_len), f32),
            vmem((rank, seq_len), f32),
            vmem((seq_len, model), f32),
            vmem((seq_len, wide), f32),
        ]
        + [vmem((seq_len, wide), f32)] * 6
        + [vmem(((seq_len + 1) * state_dim, wide), bf16)]
        + [vmem((flat, wide), bf16)] * 4
        + [vmem((blocks, state_dim, LANES), f32)] * 2
        + [vmem((seq_len, flat), bf16)] * 3
        + [vmem((seq_len, LANES), f32)] * 2
        + [vmem((2 * state_dim, seq_len), f32)]
        + [vmem((blocks, state_dim, LANES), f32)] * 6,
        name="recurrence",
        compiler_params=pltpu.CompilerParams(vmem_limit_bytes=30 * 1024 * 1024),
        cost_estimate=takes(30),
    )(keep, offs, *parts, *terms, xs, z, wo, wdt, dt_bias, skip)


def grad_of(lefts, rights):
    total = mm(lefts[0][...], rights[0][...], (0, 0))
    for left, right in zip(lefts[1:], rights[1:]):
        total = total + mm(left[...], right[...], (0, 0))
    return total


def grad_send_kernel(pairs, count, place_ref, *refs):
    out_ref = refs[2 * pairs * count]
    for g in range(pairs):
        lefts = refs[g * count : (g + 1) * count]
        rights = refs[(pairs + g) * count : (pairs + g + 1) * count]
        out_ref[g, 0] = grad_of(lefts, rights).astype(bf16)


def grad_keep_kernel(pairs, count, place_ref, *refs):
    got_ref, t1_ref, k1_ref, t2_ref, k2_ref = refs[2 * pairs * count :]
    half = t1_ref.shape[2]
    own_y = pl.program_id(0) == 1
    own_x = pl.program_id(1) == 1
    for g in range(pairs):
        lefts = refs[g * count : (g + 1) * count]
        rights = refs[(pairs + g) * count : (pairs + g + 1) * count]
        total = (grad_of(lefts, rights) + got_ref[g, 0].astype(f32)).astype(bf16)

        @pl.when(own_x)
        def _():
            k1_ref[g, 0] = total[:half]

        @pl.when(jnp.logical_not(own_x))
        def _():
            t1_ref[g, 0] = total[:half]

        @pl.when(own_y)
        def _():
            k2_ref[g, 0] = total[half:]

        @pl.when(jnp.logical_not(own_y))
        def _():
            t2_ref[g, 0] = total[half:]


def grad_mid_kernel(place_ref, k1_ref, g1_ref, k2_ref, g2_ref, o1_ref, m1_ref, o2_ref, m2_ref):
    x, y = place_ref[1], place_ref[2]
    for g in range(k1_ref.shape[0]):
        for kept, got, out, mine, own in (
            (k1_ref, g1_ref, o1_ref, m1_ref, y),
            (k2_ref, g2_ref, o2_ref, m2_ref, x),
        ):
            out[g] = (kept[g, 1 - own].astype(f32) + got[g, 1 - own].astype(f32)).astype(bf16)
            mine[g] = kept[g, own].astype(f32) + got[g, own].astype(f32)


class GradScatter:
    def __init__(self, lefts, rights, place):
        self.lefts, self.rights, self.place = lefts, rights, place
        self.pairs, self.count = len(lefts), len(lefts[0])
        self.flat = [a for pair in lefts for a in pair] + [a for pair in rights for a in pair]
        seq_len, model = lefts[0][0].shape
        self.inner = rights[0][0].shape[1]
        self.seq_len, self.rows = seq_len, model // 8

    def specs(self, index):
        n = self.pairs * self.count
        lhs = pl.BlockSpec((self.seq_len, self.rows), index)
        rhs = pl.BlockSpec((self.seq_len, self.inner), lambda *_: (0, 0))
        return [lhs] * n + [rhs] * n

    def send_core(self):
        self.got = swap(
            pl.pallas_call(
                functools.partial(grad_send_kernel, self.pairs, self.count),
                grid_spec=pltpu.PrefetchScalarGridSpec(
                    num_scalar_prefetch=1,
                    grid=(4,),
                    in_specs=self.specs(lambda j, place: (0, 2 * j + 1 - place[0])),
                    out_specs=pl.BlockSpec((self.pairs, 1, self.rows, self.inner), lambda j, place: (0, j, 0, 0)),
                ),
                out_shape=jax.ShapeDtypeStruct((self.pairs, 4, self.rows, self.inner), bf16),
                name="grad_send",
            compiler_params=pltpu.CompilerParams(vmem_limit_bytes=12 * 1024 * 1024),
                cost_estimate=takes(5.5),
            )(self.place, *self.flat),
            "dp",
            1,
        )

    def send_first(self, *behind):
        half = self.rows // 2
        shape = (self.pairs, 2, half, self.inner)
        block = (self.pairs, 1, half, self.inner)

        def at(i, own):
            return (1 - own) + i * (2 * own - 1)

        kinds = jax.ShapeDtypeStruct(shape, bf16)
        t1, self.k1, t2, self.k2 = pl.pallas_call(
            functools.partial(grad_keep_kernel, self.pairs, self.count),
            grid_spec=pltpu.PrefetchScalarGridSpec(
                num_scalar_prefetch=1,
                grid=(2, 2),
                in_specs=self.specs(lambda i, j, p: (0, 4 * at(i, p[2]) + 2 * at(j, p[1]) + p[0]))
                + [
                    pl.BlockSpec(
                        (self.pairs, 1, self.rows, self.inner),
                        lambda i, j, p: (0, 2 * at(i, p[2]) + at(j, p[1]), 0, 0),
                    )
                ],
                out_specs=[
                    pl.BlockSpec(block, lambda i, j, p: (0, at(i, p[2]), 0, 0)),
                    pl.BlockSpec(block, lambda i, j, p: (0, at(i, p[2]), 0, 0)),
                    pl.BlockSpec(block, lambda i, j, p: (0, at(jnp.maximum(i, j), p[1]), 0, 0)),
                    pl.BlockSpec(block, lambda i, j, p: (0, at(jnp.minimum(i, j), p[1]), 0, 0)),
                ],
            ),
            out_shape=[kinds] * 4,
            name="grad_keep",
            compiler_params=pltpu.CompilerParams(vmem_limit_bytes=14 * 1024 * 1024),
            cost_estimate=takes(6.5),
        )(self.place, *self.flat, after(self.got, *behind))
        self.left = self.k1
        self.g1, self.g2 = swap(t1, "dp", 2), swap(t2, "dp", 4)

    def rest(self):
        return self.left

    def send_second(self, *behind):
        half = self.rows // 2
        shape = (self.pairs, half, self.inner)
        whole = pl.BlockSpec((self.pairs, 2, half, self.inner), lambda i, p: (0, 0, 0, 0))
        part = pl.BlockSpec(shape, lambda i, p: (0, 0, 0))
        o1, self.m1, o2, self.m2 = pl.pallas_call(
            grad_mid_kernel,
            grid_spec=pltpu.PrefetchScalarGridSpec(
                num_scalar_prefetch=1, grid=(1,), in_specs=[whole] * 4, out_specs=[part] * 4
            ),
            out_shape=[jax.ShapeDtypeStruct(shape, kind) for kind in (bf16, f32, bf16, f32)],
            name="grad_mid",
            compiler_params=pltpu.CompilerParams(vmem_limit_bytes=8 * 1024 * 1024),
            cost_estimate=takes(3.5),
        )(self.place, after(self.k1, *behind), self.g1, self.k2, self.g2)
        self.left = self.m1
        self.h1, self.h2 = swap(o1, "dp", 4), swap(o2, "dp", 2)

    def finish(self, *behind):
        self.m1, self.m2, self.h1, self.h2 = after((self.m1, self.m2, self.h1, self.h2), *behind)
        return [
            jnp.concatenate([self.m1[g] + self.h1[g].astype(f32), self.m2[g] + self.h2[g].astype(f32)], 0)
            for g in range(self.pairs)
        ]


class PlainGradScatter:
    def __init__(self, lefts, rights, place):
        self.lefts, self.rights = lefts, rights

    def send_core(self):
        grads = [sum(mm(a, b, (0, 0)) for a, b in zip(left, right)) for left, right in zip(self.lefts, self.rights)]
        self.parts = [scatter_of(grad, "dp") for grad in grads]
        for part in self.parts:
            self.got = part.send()

    def send_first(self, *behind):
        for part in self.parts:
            part.add()
        for part in self.parts:
            part.send()

    send_second = send_first

    def rest(self):
        return self.parts[0].kept

    def finish(self, *behind):
        for part in self.parts:
            part.add()
        return [part.finish() for part in self.parts]


def per_device(
    states_in,
    out_cotangent,
    segments,
    starts,
    norm_gain,
    in_x_weight,
    in_z_weight,
    conv_weight,
    conv_bias,
    x_proj_weight,
    dt_weight,
    dt_bias,
    skip_weight,
    out_weight,
):
    count, rows, model = states_in.shape
    span, inner = conv_weight.shape
    rank = dt_weight.shape[0]
    seq_len = segments.shape[1]
    dp = lax.axis_size("dp")
    gain = norm_gain.astype(f32)
    proj_weight = x_proj_weight.T
    keep = 1.0 - starts[:, ::8].astype(f32)
    seqs = range(count)
    me = lax.axis_index("fsdp")
    offs = jnp.stack([(me ^ mask) * rows for mask in range(lax.axis_size("fsdp"))])[None, :].astype(jnp.int32)
    tap_bias = conv_bias[None, :]
    normed, xin, xs, z, masks, projs = [], [], [], [], [], []
    gated, gz, gxs, gprojs, small, dtg, cots, branch = [], [], [], [], [], [], [], []
    g_x_in, gn, rows_part, proj_part, gain_part = [], [], [], [], []
    tokens, cot_parts = [], []
    behind = ()
    for s in seqs:
        for source, into in ((states_in, tokens), (out_cotangent, cot_parts)):
            gather = relay_all if behind else exchange_all
            into.append(gather(after(source[s], *behind), "fsdp"))
            behind = (into[s][1],)
    for s in seqs:
        seg_ext = jnp.pad(segments[s], (span - 1, 0), constant_values=-1)
        mask = jnp.stack([(seg_ext[w : w + seq_len] == segments[s]).astype(f32) for w in range(span)], 1)
        masks.append(jnp.pad(mask, ((0, 0), (0, LANES - span))))

    def run_enter(s, *behind):
        got = enter(
            offs,
            [far(part) for part in tokens[s]],
            norm_gain[None, :],
            after(masks[s], *behind),
            far(in_x_weight),
            far(in_z_weight),
            conv_weight,
            tap_bias,
            far(proj_weight),
        )
        for into, value in zip((normed, xin, z, xs), got):
            into.append(value)
        projs.append(sum_pair(got[4], "fsdp"))

    def run_recurrence(s, *behind):
        got = recurrence(
            keep[s : s + 1],
            offs,
            [far(part) for part in cot_parts[s]],
            [far(term) for term in projs[s]],
            after(xs[s], *behind),
            z[s],
            far(out_weight),
            far(dt_weight),
            dt_bias[None, :],
            skip_weight[None, :],
        )
        for into, value in zip((gated, gz, gxs, gprojs, small, dtg, cots), got):
            into.append(value)
        gprojs[s] = sum_pair(gprojs[s], "fsdp")
        branch.append(RowScatter(*got[7:], "fsdp"))

    def run_leave(s, *behind):
        got = leave(
            offs,
            [far(term) for term in gprojs[s]],
            far(proj_weight),
            after(gxs[s], *behind),
            xin[s],
            xs[s],
            gz[s],
            masks[s],
            conv_weight,
            tap_bias,
            far(in_x_weight),
            far(in_z_weight),
            normed[s],
        )
        for into, value in zip((g_x_in, rows_part, proj_part, gain_part), got):
            into.append(value)
        gn.append(RowScatter(*got[4:], "fsdp"))

    def total_of(parts):
        total = [part.astype(f32) for part in parts]
        while len(total) > 1:
            total = [total[n] + total[n + 1] for n in range(0, len(total), 2)]
        return total[0]

    bits = [lax.rem(lax.axis_index("dp") // bit, 2) for bit in bits_of(dp)]
    place = jnp.stack(bits).astype(jnp.int32)
    scatter = GradScatter if dp == 8 and (model // dp) % 256 == 0 else PlainGradScatter
    run_enter(0)
    run_recurrence(0)
    branch[0].send()
    run_enter(1, gated[0])
    branch[0].mid()
    branch[0].send()
    run_leave(0, projs[1][0])
    gn[0].send()
    run_recurrence(1, g_x_in[0])
    branch[1].send()
    gate = (branch[0].got, gn[0].got)
    out_sum = scatter([cots], [[gated[0], after(gated[1], *gate)]], place)
    out_sum.send_core()
    z_sum = scatter([normed], [gz], place)
    z_sum.send_core()
    gn[0].mid()
    gn[0].send()
    out_sum.send_first()
    z_sum.send_first()
    branch[1].mid()
    branch[1].send()
    run_leave(1, out_sum.rest(), z_sum.rest())
    gn[1].send()
    out_sum.send_second(g_x_in[1])
    z_sum.send_second(out_sum.rest())
    x_sum = scatter([normed], [[g_x_in[0], after(g_x_in[1], z_sum.rest())]], place)
    x_sum.send_core()
    gn[1].mid()
    gn[1].send()
    x_sum.send_first()
    packed = jnp.concatenate(
        [sum(proj_part), sum(rows_part), sum(small), jnp.concatenate([sum(gain_part).reshape(-1, inner)] * 4, 0)], 0
    )
    packed = all_sum(after(packed, x_sum.rest()), "dp")
    x_sum.send_second(branch[1].got)
    gain_rows = packed[proj_weight.shape[0] + 16 : proj_weight.shape[0] + 16 + model // inner]
    gain_grad = total_of(exchange_all(gain_rows, "fsdp")).reshape(-1) / gain
    (out_grad,), (in_z_grad,), (in_x_grad,) = out_sum.finish(x_sum.rest()), z_sum.finish(x_sum.rest()), x_sum.finish()
    outputs, input_grads = [], []
    for s in seqs:
        v = after(states_in[s], x_sum.rest()).astype(f32)
        outputs.append((v + branch[s].finish()).astype(bf16))
        rscale = lax.rsqrt(jnp.mean(v * v, axis=1, keepdims=True) + norm_eps)
        scaled = gn[s].finish() * gain
        inner_mean = jnp.mean(scaled * v, axis=1, keepdims=True)
        input_grads.append(out_cotangent[s].astype(f32) + rscale * scaled - v * (rscale * rscale * rscale) * inner_mean)
    dt_grad = scatter_of(after(sum(dtg), x_sum.rest()), "dp").finish()
    tail = packed[proj_weight.shape[0] :]
    return (
        jnp.stack(outputs),
        jnp.stack(input_grads),
        gain_grad,
        in_x_grad,
        in_z_grad,
        tail[:span],
        tail[span],
        packed[: proj_weight.shape[0]].T,
        dt_grad,
        tail[8 + 1],
        tail[8],
        out_grad.T,
    )


def solution(mesh):
    in_specs = (
        P("dp", "fsdp", None),
        P("dp", "fsdp", None),
        P("dp", None),
        P("dp", None),
        P(),
        P(None, "fsdp"),
        P(None, "fsdp"),
        P(None, "fsdp"),
        P("fsdp"),
        P("fsdp", None),
        P(None, "fsdp"),
        P("fsdp"),
        P("fsdp"),
        P("fsdp", None),
    )
    out_specs = (
        P("dp", "fsdp", None),
        P("dp", "fsdp", None),
        P(),
        P("dp", "fsdp"),
        P("dp", "fsdp"),
        P(None, "fsdp"),
        P("fsdp"),
        P("fsdp", None),
        P("dp", "fsdp"),
        P("fsdp"),
        P("fsdp"),
        P("fsdp", "dp"),
    )
    return jax.shard_map(per_device, mesh=mesh, in_specs=in_specs, out_specs=out_specs, check_vma=False)
```

```python
import functools

import jax
import jax.numpy as jnp
from jax import lax
from jax.experimental import pallas as pl
from jax.experimental.pallas import tpu as pltpu
from jax.sharding import PartitionSpec as P

BLOCK = 16
LANES = 128
norm_eps = 1e-05


def takes(microseconds):
    return pl.CostEstimate(flops=int(microseconds * 9e8), bytes_accessed=1, transcendentals=0)
f32 = jnp.float32
bf16 = jnp.bfloat16


def mm(left, right, contract):
    return lax.dot_general(left, right, ((contract[:1], contract[1:]), ((), ())), preferred_element_type=f32)


def swap(x, axis, bit):
    return lax.ppermute(x, axis, [(i, i ^ bit) for i in range(lax.axis_size(axis))])


def bits_of(count):
    return [1 << k for k in range(count.bit_length() - 1)]


def exchange_all(x, axis):
    return [x] + [swap(x, axis, mask) for mask in range(1, lax.axis_size(axis))]


def relay_all(x, axis):
    held = {0: x}
    for bit in reversed(bits_of(lax.axis_size(axis))):
        for mask in list(held):
            held[mask | bit] = swap(held[mask], axis, bit)
    return [held[mask] for mask in range(len(held))]


class RowScatter:
    def __init__(self, sent, kept, axis):
        self.axis, self.bits = axis, bits_of(lax.axis_size(axis))
        self.sent, self.kept = sent, kept

    def send(self, *behind):
        self.got = swap(after(self.sent, *behind), self.axis, self.bits.pop(0))

    def mid(self):
        self.sent = (self.kept[1::2].astype(f32) + self.got[1::2].astype(f32)).astype(bf16)
        self.kept = (self.kept[0::2].astype(f32) + self.got[0::2].astype(f32))

    def finish(self):
        while self.bits:
            self.mid()
            self.send()
        return self.kept[0].astype(f32) + self.got[0].astype(f32)


def after(x, *others):
    return lax.optimization_barrier((x, others))[0] if others else x


def sum_pair(x, axis):
    bits = bits_of(lax.axis_size(axis))
    for bit in bits[:-1]:
        x = (x.astype(f32) + swap(x, axis, bit).astype(f32)).astype(bf16)
    return [x, swap(x, axis, bits[-1])]


def take_bit(x, dim, value):
    return lax.dynamic_index_in_dim(x, value, dim, keepdims=False)


class Scatter:
    def __init__(self, x, axis, bits, dims):
        self.x, self.axis, self.left = x, axis, list(zip(bits, dims))

    def send(self):
        bit, dim = self.left[0]
        own = (lax.axis_index(self.axis) // bit) % 2
        self.got = swap(take_bit(self.x, dim, 1 - own).astype(bf16), self.axis, bit)
        self.kept = take_bit(self.x, dim, own)
        return self.got

    def add(self):
        _, dim = self.left.pop(0)
        self.left = [(bit, d - 1 if d > dim else d) for bit, d in self.left]
        self.x = self.kept.astype(f32) + self.got.astype(f32)

    def finish(self):
        while self.left:
            self.send()
            self.add()
        return self.x


def scatter_of(x, axis):
    count = lax.axis_size(axis)
    bits = bits_of(count)
    n = len(bits)
    return Scatter(x.reshape((2,) * n + (x.shape[0] // count,) + x.shape[1:]), axis, bits, range(n - 1, -1, -1))


def all_sum(x, axis, kind=bf16):
    for bit in bits_of(lax.axis_size(axis)):
        low = x.astype(kind)
        x = low.astype(f32) + swap(low, axis, bit).astype(f32)
    return x


def far(x):
    return pltpu.with_memory_space_constraint(x, pltpu.HBM)


def add_up(refs):
    total = refs[0][...].astype(f32)
    for ref in refs[1:]:
        total = total + ref[...].astype(f32)
    return total


def silu_slope(v):
    s = jax.nn.sigmoid(v)
    return s * (1.0 + v * (1.0 - s))


def conv_sum(x, masks, taps, bias):
    span = taps.shape[0]
    total = bias + taps[span - 1 : span] * x
    shifted = []
    for w in range(span - 1):
        moved = pltpu.roll(x, span - 1 - w, 0) * masks[:, w : w + 1]
        shifted.append(moved)
        total = total + taps[w : w + 1] * moved
    return total, shifted + [x]


def enter_kernel(count, offs_ref, *refs):
    parts = refs[:count]
    gain_ref, mask_ref, wx_ref, wz_ref, taps_ref, bias_ref, wp_ref = refs[count : count + 7]
    normed_ref, xin_ref, z_ref, xs_ref, proj_ref, acc_s = refs[count + 7 :]
    step = pl.program_id(0)

    @pl.when(step == 0)
    def _():
        gain = gain_ref[...].astype(f32)
        for m, part in enumerate(parts):
            v = part[...].astype(f32)
            rscale = lax.rsqrt(jnp.mean(v * v, axis=1, keepdims=True) + norm_eps)
            rows = part.shape[0]
            normed_ref[pl.ds(pl.multiple_of(offs_ref[0, m], rows), rows), :] = (v * rscale * gain).astype(bf16)
        acc_s[...] = jnp.zeros_like(acc_s)

    normed = normed_ref[...]
    z_ref[...] = jnp.dot(normed, wz_ref[...], preferred_element_type=f32)
    x_in = jnp.dot(normed, wx_ref[...], preferred_element_type=f32).astype(bf16)
    xin_ref[...] = x_in
    pre, _ = conv_sum(x_in.astype(f32), mask_ref[...], taps_ref[...].astype(f32), bias_ref[...].astype(f32))
    xs = jax.nn.silu(pre).astype(bf16)
    xs_ref[...] = xs
    acc_s[...] += mm(wp_ref[...], xs, (1, 1))

    @pl.when(step == pl.num_programs(0) - 1)
    def _():
        proj_ref[...] = acc_s[...].astype(bf16)


def blocks_of(rows, wide):
    return pl.BlockSpec((rows, wide), lambda c: (0, c))


def whole_of(shape):
    return pl.BlockSpec(shape, lambda c: (0,) * len(shape))


def enter(offs, parts, gain, masks, wx, wz, taps, bias, wp):
    rows, model = parts[0].shape
    seq_len = rows * len(parts)
    inner = wx.shape[1]
    wide = 512
    return pl.pallas_call(
        functools.partial(enter_kernel, len(parts)),
        grid=(inner // wide,),
        in_specs=[pl.BlockSpec(memory_space=pltpu.SMEM)]
        + [whole_of((rows, model))] * len(parts)
        + [
            whole_of((1, model)),
            whole_of(masks.shape),
            blocks_of(model, wide),
            blocks_of(model, wide),
            blocks_of(taps.shape[0], wide),
            blocks_of(1, wide),
            blocks_of(wp.shape[0], wide),
        ],
        out_specs=[
            whole_of((seq_len, model)),
            blocks_of(seq_len, wide),
            blocks_of(seq_len, wide),
            blocks_of(seq_len, wide),
            whole_of((wp.shape[0], seq_len)),
        ],
        out_shape=[
            jax.ShapeDtypeStruct((seq_len, model), bf16),
            jax.ShapeDtypeStruct((seq_len, inner), bf16),
            jax.ShapeDtypeStruct((seq_len, inner), f32),
            jax.ShapeDtypeStruct((seq_len, inner), bf16),
            jax.ShapeDtypeStruct((wp.shape[0], seq_len), bf16),
        ],
        scratch_shapes=[pltpu.VMEM((wp.shape[0], seq_len), f32)],
        name="enter",
        compiler_params=pltpu.CompilerParams(vmem_limit_bytes=28 * 1024 * 1024),
        cost_estimate=takes(9),
    )(offs, *parts, gain, masks, wx, wz, taps, bias, wp)


def write_parts(offs_ref, total_s, sent_ref, kept_ref):
    count, rows = kept_ref.shape[0], kept_ref.shape[1]
    for m in range(count):
        for odd, out in ((0, kept_ref), (1, sent_ref)):
            off = pl.multiple_of(offs_ref[0, 2 * m + odd], rows)
            out[m] = total_s[pl.ds(off, rows), :].astype(bf16)


def leave_kernel(count, offs_ref, *refs):
    terms = refs[:count]
    wp_ref, gxs_ref, xin_ref, xs_ref, gz_ref, mask_ref, taps_ref, bias_ref, wx_ref, wz_ref, normed_ref = refs[
        count : count + 11
    ]
    gxin_ref, rows_ref, xpg_ref, gain_ref = refs[count + 11 : count + 15]
    sent_ref, kept_ref, acc_s = refs[count + 15 :]
    step = pl.program_id(0)
    span = taps_ref.shape[0]
    seq_len = xin_ref.shape[0]
    gproj = add_up(terms).astype(bf16)
    xpg_ref[...] = mm(gproj, xs_ref[...], (1, 0))
    g_xs = gxs_ref[...] + mm(gproj, wp_ref[...], (0, 0))
    masks = mask_ref[...]
    taps = taps_ref[...].astype(f32)
    pre, shifted = conv_sum(xin_ref[...].astype(f32), masks, taps, bias_ref[...].astype(f32))
    g_conv = g_xs * silu_slope(pre)
    total = taps[span - 1 : span] * g_conv
    for w in range(span):
        rows_ref[w : w + 1, :] = jnp.sum(g_conv * shifted[w], axis=0, keepdims=True)
        if w < span - 1:
            term = g_conv * masks[:, w : w + 1] * taps[w : w + 1]
            total = total + pltpu.roll(term, seq_len - (span - 1 - w), 0)
    rows_ref[span : span + 1, :] = jnp.sum(g_conv, axis=0, keepdims=True)
    rows_ref[span + 1 :, :] = jnp.zeros((8 - span - 1, g_conv.shape[1]), f32)
    g_x_in = total.astype(bf16)
    gxin_ref[...] = g_x_in
    gn = mm(g_x_in, wx_ref[...], (1, 1)) + mm(gz_ref[...], wz_ref[...], (1, 1))

    @pl.when(step == 0)
    def _():
        acc_s[...] = gn

    @pl.when(step > 0)
    def _():
        acc_s[...] += gn

    @pl.when(step == pl.num_programs(0) - 1)
    def _():
        gn = acc_s[...]
        write_parts(offs_ref, acc_s, sent_ref, kept_ref)
        gain_ref[...] = jnp.sum(gn * normed_ref[...].astype(f32), axis=0, keepdims=True)


def leave(offs, terms, wp, gxs, xin, xs, gz, masks, taps, bias, wx, wz, normed):
    seq_len, model = normed.shape
    inner = wx.shape[1]
    count = offs.shape[1]
    wide = 256
    return pl.pallas_call(
        functools.partial(leave_kernel, len(terms)),
        grid=(inner // wide,),
        in_specs=[pl.BlockSpec(memory_space=pltpu.SMEM)]
        + [whole_of(terms[0].shape)] * len(terms)
        + [
            blocks_of(wp.shape[0], wide),
            blocks_of(seq_len, wide),
            blocks_of(seq_len, wide),
            blocks_of(seq_len, wide),
            blocks_of(seq_len, wide),
            whole_of(masks.shape),
            blocks_of(taps.shape[0], wide),
            blocks_of(1, wide),
            blocks_of(model, wide),
            blocks_of(model, wide),
            whole_of((seq_len, model)),
        ],
        out_specs=[
            blocks_of(seq_len, wide),
            blocks_of(8, wide),
            blocks_of(wp.shape[0], wide),
            whole_of((1, model)),
        ]
        + [whole_of((count // 2, seq_len // count, model))] * 2,
        out_shape=[
            jax.ShapeDtypeStruct((seq_len, inner), bf16),
            jax.ShapeDtypeStruct((8, inner), f32),
            jax.ShapeDtypeStruct((wp.shape[0], inner), f32),
            jax.ShapeDtypeStruct((1, model), f32),
        ]
        + [jax.ShapeDtypeStruct((count // 2, seq_len // count, model), bf16)] * 2,
        scratch_shapes=[pltpu.VMEM((seq_len, model), f32)],
        name="leave",
        compiler_params=pltpu.CompilerParams(vmem_limit_bytes=24 * 1024 * 1024),
        cost_estimate=takes(10),
    )(offs, *terms, wp, gxs, xin, xs, gz, masks, taps, bias, wx, wz, normed)


def recurrence_kernel(state_dim, rank, count, keep_ref, offs_ref, *refs):
    parts, terms, refs = refs[:count], refs[count : count + 2], refs[count + 2 :]
    xs_ref, z_ref, wo_ref, wdt_ref, dtb_ref, skip_ref = refs[:6]
    gated_ref, gz_ref, gxs_ref, gproj_ref, small_ref, dtg_ref, cot_ref, sent_ref, kept_ref = refs[6:15]
    (
        gg_s,
        proj_s,
        gproj_s,
        acc_s,
        slope_s,
        eps_s,
        u_s,
        gm_s,
        y_s,
        s1_s,
        s2_s,
        hist_s,
        even_g_s,
        odd_g_s,
        even_p_s,
        odd_p_s,
        kt_s,
        qt_s,
        kd_s,
        k2d_s,
        qd_s,
        norm_s,
        sum_s,
        tail_s,
        gq_s,
        ge_s,
        pe_s,
        gqt_s,
        get_s,
        pet_s,
    ) = refs[15:]
    step = pl.program_id(0)
    seq_len, width = xs_ref.shape
    blocks = seq_len // BLOCK
    flat = BLOCK * state_dim
    lane = lax.broadcasted_iota(jnp.int32, (state_dim, BLOCK), 1)

    @pl.when(step == 0)
    def _():
        proj_s[...] = add_up(terms)
        for m, part in enumerate(parts):
            rows = part.shape[0]
            cot_ref[pl.ds(pl.multiple_of(offs_ref[0, m], rows), rows), :] = part[...]
        turned = proj_s[rank:, :]
        for b in range(blocks):
            cols = slice(b * BLOCK, (b + 1) * BLOCK)
            kt_s[b] = jnp.pad(turned[:state_dim, cols], ((0, 0), (0, LANES - BLOCK)))
            qt_s[b] = jnp.pad(turned[state_dim:, cols], ((0, 0), (0, LANES - BLOCK)))
        source = lax.broadcasted_iota(jnp.int32, (2 * state_dim, flat), 0)
        target = lax.rem(lax.broadcasted_iota(jnp.int32, (2 * state_dim, flat), 1), state_dim)
        take_k = (source == target).astype(bf16)
        take_q = (source == target + state_dim).astype(bf16)
        own = (
            lax.rem(lax.broadcasted_iota(jnp.int32, (seq_len, flat), 0), BLOCK)
            == lax.broadcasted_iota(jnp.int32, (seq_len, flat), 1) // state_dim
        )
        kd_s[...] = jnp.where(own, mm(turned.astype(bf16), take_k, (0, 0)), 0.0).astype(bf16)
        k2d_s[...] = jnp.where(own, mm((turned * turned).astype(bf16), take_k, (0, 0)), 0.0).astype(bf16)
        qd_s[...] = jnp.where(own, mm(turned.astype(bf16), take_q, (0, 0)), 0.0).astype(bf16)
        square = jnp.sum(turned[:state_dim] * turned[:state_dim], axis=0, keepdims=True)
        norm_s[...] = jnp.broadcast_to(square, (LANES, seq_len)).T
        sum_s[...] = jnp.zeros_like(sum_s)
        gq_s[...] = jnp.zeros_like(gq_s)
        ge_s[...] = jnp.zeros_like(ge_s)
        pe_s[...] = jnp.zeros_like(pe_s)

    gg_s[...] = mm(cot_ref[...], wo_ref[...], (1, 1))
    low = proj_s[:rank, :].astype(bf16)
    dt_pre = mm(low, wdt_ref[...], (0, 0)) + dtb_ref[...].astype(f32)
    rates = jnp.maximum(dt_pre, 0.0) + jnp.log1p(jnp.exp(-jnp.abs(dt_pre)))
    ratio = 1.0 / (1.0 + rates * norm_s[:, 0:1])
    eps_s[...] = rates * ratio
    slope_s[...] = ratio * ratio * jax.nn.sigmoid(dt_pre)
    u_s[...] = eps_s[...] * xs_ref[...].astype(f32)
    gm_s[...] = gg_s[...] * jax.nn.silu(z_ref[...])
    hist_s[0:state_dim, :] = jnp.zeros((state_dim, width), bf16)

    def own_token(pairs):
        picked = pairs[:state_dim]
        for t in range(1, BLOCK):
            picked = jnp.where(lane == t, pairs[t * state_dim : (t + 1) * state_dim], picked)
        return picked

    def read_states(b, buf):
        toks = pl.ds(pl.multiple_of(b * BLOCK, BLOCK), BLOCK)
        hblk = buf[...]
        y_s[toks, :] = jnp.dot(qd_s[toks, :], hblk, preferred_element_type=f32)
        gqt_s[b, :, :BLOCK] = own_token(mm(hblk, gm_s[toks, :].astype(bf16), (1, 1)))

    def scan_block(b, h, buf):
        base = pl.multiple_of(b * BLOCK, BLOCK)
        kt = kt_s[b]
        for t in range(BLOCK):
            if t % 8 == 0:
                h = h * keep_ref[0, b * 2 + t // 8]
            col = jnp.broadcast_to(kt[:, t : t + 1], (state_dim, width))
            e = eps_s[pl.ds(base + t, 1), :]
            u = u_s[pl.ds(base + t, 1), :]
            h = (1.0 - (col * col) * e) * h + col * u
            kept = h.astype(bf16)
            hist_s[pl.ds(pl.multiple_of((base + t + 1) * state_dim, state_dim), state_dim), :] = kept
            buf[t * state_dim : (t + 1) * state_dim, :] = kept
        return h

    def forward(i, h):
        read_states(jnp.maximum(2 * i - 1, 0), odd_g_s)
        h = scan_block(2 * i, h, even_g_s)
        read_states(2 * i, even_g_s)
        return scan_block(2 * i + 1, h, odd_g_s)

    lax.fori_loop(0, blocks // 2, forward, jnp.zeros((state_dim, width), f32))
    read_states(blocks - 1, odd_g_s)

    def read_grads(b, gbuf, pbuf):
        toks = pl.ds(pl.multiple_of(b * BLOCK, BLOCK), BLOCK)
        gblk = gbuf[...]
        pblk = pbuf[...]
        s1_s[toks, :] = jnp.dot(kd_s[toks, :], gblk, preferred_element_type=f32)
        s2_s[toks, :] = jnp.dot(k2d_s[toks, :], pblk, preferred_element_type=f32)
        get_s[b, :, :BLOCK] = own_token(mm(gblk, u_s[toks, :].astype(bf16), (1, 1)))
        pet_s[b, :, :BLOCK] = own_token(mm(pblk, eps_s[toks, :].astype(bf16), (1, 1)))

    def back_block(b, carry, gbuf, pbuf):
        base = pl.multiple_of(b * BLOCK, BLOCK)
        kt = kt_s[b]
        qt = qt_s[b]
        for t in reversed(range(BLOCK)):
            colq = jnp.broadcast_to(qt[:, t : t + 1], (state_dim, width))
            col = jnp.broadcast_to(kt[:, t : t + 1], (state_dim, width))
            e = eps_s[pl.ds(base + t, 1), :]
            gm = gm_s[pl.ds(base + t, 1), :]
            g = colq * gm + carry
            before = hist_s[pl.ds(pl.multiple_of((base + t) * state_dim, state_dim), state_dim), :].astype(f32)
            p = g * before
            carry = (1.0 - (col * col) * e) * g
            if t % 8 == 0:
                k = keep_ref[0, b * 2 + t // 8]
                carry = carry * k
                p = p * k
            gbuf[t * state_dim : (t + 1) * state_dim, :] = g.astype(bf16)
            pbuf[t * state_dim : (t + 1) * state_dim, :] = p.astype(bf16)
        return carry

    def backward(i, carry):
        last = blocks - 1 - 2 * i
        read_grads(jnp.minimum(last + 1, blocks - 1), even_g_s, even_p_s)
        carry = back_block(last, carry, odd_g_s, odd_p_s)
        read_grads(last, odd_g_s, odd_p_s)
        return back_block(last - 1, carry, even_g_s, even_p_s)

    lax.fori_loop(0, blocks // 2, backward, jnp.zeros((state_dim, width), f32))
    read_grads(0, even_g_s, even_p_s)
    gq_s[...] += gqt_s[...]
    ge_s[...] += get_s[...]
    pe_s[...] += pet_s[...]

    xs = xs_ref[...].astype(f32)
    z = z_ref[...]
    skip = skip_ref[...].astype(f32)
    sig = jax.nn.sigmoid(z)
    mixed = y_s[...] + skip * xs
    gated = (mixed * (z * sig)).astype(bf16)
    gated_ref[...] = gated
    out_part = jnp.dot(gated, wo_ref[...], preferred_element_type=f32)
    gz_ref[...] = (gg_s[...] * mixed * (sig * (1.0 + z * (1.0 - sig)))).astype(bf16)
    gm = gm_s[...]
    s1 = s1_s[...]
    eps = eps_s[...]
    g_eps = xs * s1 - s2_s[...]
    sum_s[...] += jnp.broadcast_to(jnp.sum(g_eps * eps * eps, axis=1, keepdims=True), sum_s.shape)
    g_dt = (g_eps * slope_s[...]).astype(bf16)
    dtg_ref[...] = mm(low, g_dt, (1, 0))
    gxs_ref[...] = skip * gm + eps * s1
    small_ref[0:1, :] = jnp.sum(gm * xs, axis=0, keepdims=True)
    small_ref[1:2, :] = jnp.sum(g_dt.astype(f32), axis=0, keepdims=True)
    small_ref[2:, :] = jnp.zeros((6, width), f32)
    g_low = mm(wdt_ref[...], g_dt, (1, 1))

    @pl.when(step == 0)
    def _():
        gproj_s[...] = g_low
        acc_s[...] = out_part

    @pl.when(step > 0)
    def _():
        gproj_s[...] += g_low
        acc_s[...] += out_part

    @pl.when(step == pl.num_programs(0) - 1)
    def _():
        scale = sum_s[...].T[0:1, :]
        for b in range(blocks):
            cols = slice(b * BLOCK, (b + 1) * BLOCK)
            own_keys = ge_s[b, :, :BLOCK] - 2.0 * kt_s[b, :, :BLOCK] * (pe_s[b, :, :BLOCK] + scale[:, cols])
            tail_s[:state_dim, cols] = own_keys
            tail_s[state_dim:, cols] = gq_s[b, :, :BLOCK]
        gproj_ref[:rank, :] = gproj_s[...].astype(bf16)
        gproj_ref[rank:, :] = tail_s[...].astype(bf16)
        write_parts(offs_ref, acc_s, sent_ref, kept_ref)


def recurrence(keep, offs, parts, terms, xs, z, wo, wdt, dt_bias, skip):
    seq_len, inner = xs.shape
    model = wo.shape[1]
    rank = wdt.shape[0]
    columns = terms[0].shape[0]
    state_dim = (columns - rank) // 2
    wide = 512
    flat = BLOCK * state_dim
    blocks = seq_len // BLOCK
    vmem = pltpu.VMEM
    return pl.pallas_call(
        functools.partial(recurrence_kernel, state_dim, rank, len(parts)),
        grid=(inner // wide,),
        in_specs=[pl.BlockSpec(memory_space=pltpu.SMEM)] * 2
        + [whole_of(parts[0].shape)] * len(parts)
        + [whole_of((columns, seq_len))] * len(terms)
        + [
            blocks_of(seq_len, wide),
            blocks_of(seq_len, wide),
            pl.BlockSpec((wide, model), lambda c: (c, 0)),
            blocks_of(rank, wide),
            blocks_of(1, wide),
            blocks_of(1, wide),
        ],
        out_specs=[
            blocks_of(seq_len, wide),
            blocks_of(seq_len, wide),
            blocks_of(seq_len, wide),
            whole_of((columns, seq_len)),
            blocks_of(8, wide),
            blocks_of(rank, wide),
            whole_of((seq_len, model)),
        ]
        + [whole_of((len(parts) // 2,) + parts[0].shape)] * 2,
        out_shape=[
            jax.ShapeDtypeStruct((seq_len, inner), bf16),
            jax.ShapeDtypeStruct((seq_len, inner), bf16),
            jax.ShapeDtypeStruct((seq_len, inner), f32),
            jax.ShapeDtypeStruct((columns, seq_len), bf16),
            jax.ShapeDtypeStruct((8, inner), f32),
            jax.ShapeDtypeStruct((rank, inner), f32),
            jax.ShapeDtypeStruct((seq_len, model), bf16),
        ]
        + [jax.ShapeDtypeStruct((len(parts) // 2,) + parts[0].shape, bf16)] * 2,
        scratch_shapes=[
            vmem((seq_len, wide), f32),
            vmem((columns, seq_len), f32),
            vmem((rank, seq_len), f32),
            vmem((seq_len, model), f32),
            vmem((seq_len, wide), f32),
        ]
        + [vmem((seq_len, wide), f32)] * 6
        + [vmem(((seq_len + 1) * state_dim, wide), bf16)]
        + [vmem((flat, wide), bf16)] * 4
        + [vmem((blocks, state_dim, LANES), f32)] * 2
        + [vmem((seq_len, flat), bf16)] * 3
        + [vmem((seq_len, LANES), f32)] * 2
        + [vmem((2 * state_dim, seq_len), f32)]
        + [vmem((blocks, state_dim, LANES), f32)] * 6,
        name="recurrence",
        compiler_params=pltpu.CompilerParams(vmem_limit_bytes=30 * 1024 * 1024),
        cost_estimate=takes(30),
    )(keep, offs, *parts, *terms, xs, z, wo, wdt, dt_bias, skip)


def grad_of(lefts, rights):
    total = mm(lefts[0][...], rights[0][...], (0, 0))
    for left, right in zip(lefts[1:], rights[1:]):
        total = total + mm(left[...], right[...], (0, 0))
    return total


def grad_send_kernel(pairs, count, place_ref, *refs):
    out_ref = refs[2 * pairs * count]
    for g in range(pairs):
        lefts = refs[g * count : (g + 1) * count]
        rights = refs[(pairs + g) * count : (pairs + g + 1) * count]
        out_ref[g, 0] = grad_of(lefts, rights).astype(bf16)


def grad_keep_kernel(pairs, count, place_ref, *refs):
    got_ref, t1_ref, k1_ref, t2_ref, k2_ref = refs[2 * pairs * count :]
    half = t1_ref.shape[2]
    own_y = pl.program_id(0) == 1
    own_x = pl.program_id(1) == 1
    for g in range(pairs):
        lefts = refs[g * count : (g + 1) * count]
        rights = refs[(pairs + g) * count : (pairs + g + 1) * count]
        total = (grad_of(lefts, rights) + got_ref[g, 0].astype(f32)).astype(bf16)

        @pl.when(own_x)
        def _():
            k1_ref[g, 0] = total[:half]

        @pl.when(jnp.logical_not(own_x))
        def _():
            t1_ref[g, 0] = total[:half]

        @pl.when(own_y)
        def _():
            k2_ref[g, 0] = total[half:]

        @pl.when(jnp.logical_not(own_y))
        def _():
            t2_ref[g, 0] = total[half:]


def grad_mid_kernel(place_ref, k1_ref, g1_ref, k2_ref, g2_ref, o1_ref, m1_ref, o2_ref, m2_ref):
    x, y = place_ref[1], place_ref[2]
    for g in range(k1_ref.shape[0]):
        for kept, got, out, mine, own in (
            (k1_ref, g1_ref, o1_ref, m1_ref, y),
            (k2_ref, g2_ref, o2_ref, m2_ref, x),
        ):
            out[g] = (kept[g, 1 - own].astype(f32) + got[g, 1 - own].astype(f32)).astype(bf16)
            mine[g] = kept[g, own].astype(f32) + got[g, own].astype(f32)


class GradScatter:
    def __init__(self, lefts, rights, place):
        self.lefts, self.rights, self.place = lefts, rights, place
        self.pairs, self.count = len(lefts), len(lefts[0])
        self.flat = [a for pair in lefts for a in pair] + [a for pair in rights for a in pair]
        seq_len, model = lefts[0][0].shape
        self.inner = rights[0][0].shape[1]
        self.seq_len, self.rows = seq_len, model // 8

    def specs(self, index):
        n = self.pairs * self.count
        lhs = pl.BlockSpec((self.seq_len, self.rows), index)
        rhs = pl.BlockSpec((self.seq_len, self.inner), lambda *_: (0, 0))
        return [lhs] * n + [rhs] * n

    def send_core(self):
        self.got = swap(
            pl.pallas_call(
                functools.partial(grad_send_kernel, self.pairs, self.count),
                grid_spec=pltpu.PrefetchScalarGridSpec(
                    num_scalar_prefetch=1,
                    grid=(4,),
                    in_specs=self.specs(lambda j, place: (0, 2 * j + 1 - place[0])),
                    out_specs=pl.BlockSpec((self.pairs, 1, self.rows, self.inner), lambda j, place: (0, j, 0, 0)),
                ),
                out_shape=jax.ShapeDtypeStruct((self.pairs, 4, self.rows, self.inner), bf16),
                name="grad_send",
            compiler_params=pltpu.CompilerParams(vmem_limit_bytes=12 * 1024 * 1024),
                cost_estimate=takes(5.5),
            )(self.place, *self.flat),
            "dp",
            1,
        )

    def send_first(self, *behind):
        half = self.rows // 2
        shape = (self.pairs, 2, half, self.inner)
        block = (self.pairs, 1, half, self.inner)

        def at(i, own):
            return (1 - own) + i * (2 * own - 1)

        kinds = jax.ShapeDtypeStruct(shape, bf16)
        t1, self.k1, t2, self.k2 = pl.pallas_call(
            functools.partial(grad_keep_kernel, self.pairs, self.count),
            grid_spec=pltpu.PrefetchScalarGridSpec(
                num_scalar_prefetch=1,
                grid=(2, 2),
                in_specs=self.specs(lambda i, j, p: (0, 4 * at(i, p[2]) + 2 * at(j, p[1]) + p[0]))
                + [
                    pl.BlockSpec(
                        (self.pairs, 1, self.rows, self.inner),
                        lambda i, j, p: (0, 2 * at(i, p[2]) + at(j, p[1]), 0, 0),
                    )
                ],
                out_specs=[
                    pl.BlockSpec(block, lambda i, j, p: (0, at(i, p[2]), 0, 0)),
                    pl.BlockSpec(block, lambda i, j, p: (0, at(i, p[2]), 0, 0)),
                    pl.BlockSpec(block, lambda i, j, p: (0, at(jnp.maximum(i, j), p[1]), 0, 0)),
                    pl.BlockSpec(block, lambda i, j, p: (0, at(jnp.minimum(i, j), p[1]), 0, 0)),
                ],
            ),
            out_shape=[kinds] * 4,
            name="grad_keep",
            compiler_params=pltpu.CompilerParams(vmem_limit_bytes=14 * 1024 * 1024),
            cost_estimate=takes(6.5),
        )(self.place, *self.flat, after(self.got, *behind))
        self.left = self.k1
        self.g1, self.g2 = swap(t1, "dp", 2), swap(t2, "dp", 4)

    def rest(self):
        return self.left

    def send_second(self, *behind):
        half = self.rows // 2
        shape = (self.pairs, half, self.inner)
        whole = pl.BlockSpec((self.pairs, 2, half, self.inner), lambda i, p: (0, 0, 0, 0))
        part = pl.BlockSpec(shape, lambda i, p: (0, 0, 0))
        o1, self.m1, o2, self.m2 = pl.pallas_call(
            grad_mid_kernel,
            grid_spec=pltpu.PrefetchScalarGridSpec(
                num_scalar_prefetch=1, grid=(1,), in_specs=[whole] * 4, out_specs=[part] * 4
            ),
            out_shape=[jax.ShapeDtypeStruct(shape, kind) for kind in (bf16, f32, bf16, f32)],
            name="grad_mid",
            compiler_params=pltpu.CompilerParams(vmem_limit_bytes=8 * 1024 * 1024),
            cost_estimate=takes(3.5),
        )(self.place, after(self.k1, *behind), self.g1, self.k2, self.g2)
        self.left = self.m1
        self.h1, self.h2 = swap(o1, "dp", 4), swap(o2, "dp", 2)

    def finish(self, *behind):
        self.m1, self.m2, self.h1, self.h2 = after((self.m1, self.m2, self.h1, self.h2), *behind)
        return [
            jnp.concatenate([self.m1[g] + self.h1[g].astype(f32), self.m2[g] + self.h2[g].astype(f32)], 0)
            for g in range(self.pairs)
        ]


class PlainGradScatter:
    h1 = h2 = ()

    def __init__(self, lefts, rights, place):
        self.lefts, self.rights = lefts, rights

    def send_core(self):
        grads = [sum(mm(a, b, (0, 0)) for a, b in zip(left, right)) for left, right in zip(self.lefts, self.rights)]
        self.parts = [scatter_of(grad, "dp") for grad in grads]
        for part in self.parts:
            self.got = part.send()

    def send_first(self, *behind):
        for part in self.parts:
            part.add()
        for part in self.parts:
            part.send()

    send_second = send_first

    def rest(self):
        return self.parts[0].kept

    def finish(self, *behind):
        for part in self.parts:
            part.add()
        return [part.finish() for part in self.parts]


def per_device(
    states_in,
    out_cotangent,
    segments,
    starts,
    norm_gain,
    in_x_weight,
    in_z_weight,
    conv_weight,
    conv_bias,
    x_proj_weight,
    dt_weight,
    dt_bias,
    skip_weight,
    out_weight,
):
    count, rows, model = states_in.shape
    span, inner = conv_weight.shape
    rank = dt_weight.shape[0]
    seq_len = segments.shape[1]
    dp = lax.axis_size("dp")
    gain = norm_gain.astype(f32)
    proj_weight = x_proj_weight.T
    keep = 1.0 - starts[:, ::8].astype(f32)
    seqs = range(count)
    me = lax.axis_index("fsdp")
    offs = jnp.stack([(me ^ mask) * rows for mask in range(lax.axis_size("fsdp"))])[None, :].astype(jnp.int32)
    tap_bias = conv_bias[None, :]
    normed, xin, xs, z, masks, projs = [], [], [], [], [], []
    gated, gz, gxs, gprojs, small, dtg, cots, branch = [], [], [], [], [], [], [], []
    g_x_in, gn, rows_part, proj_part, gain_part = [], [], [], [], []
    tokens, cot_parts = [], []
    behind = ()
    for s in seqs:
        for source, into in ((states_in, tokens), (out_cotangent, cot_parts)):
            gather = relay_all if behind else exchange_all
            into.append(gather(after(source[s], *behind), "fsdp"))
            behind = (into[s][1],)
    for s in seqs:
        seg_ext = jnp.pad(segments[s], (span - 1, 0), constant_values=-1)
        mask = jnp.stack([(seg_ext[w : w + seq_len] == segments[s]).astype(f32) for w in range(span)], 1)
        masks.append(jnp.pad(mask, ((0, 0), (0, LANES - span))))

    def run_enter(s, *behind):
        got = enter(
            offs,
            [far(part) for part in tokens[s]],
            norm_gain[None, :],
            after(masks[s], *behind),
            far(in_x_weight),
            far(in_z_weight),
            conv_weight,
            tap_bias,
            far(proj_weight),
        )
        for into, value in zip((normed, xin, z, xs), got):
            into.append(value)
        projs.append(sum_pair(got[4], "fsdp"))

    def run_recurrence(s, *behind):
        got = recurrence(
            keep[s : s + 1],
            offs,
            [far(part) for part in cot_parts[s]],
            [far(term) for term in projs[s]],
            after(xs[s], *behind),
            z[s],
            far(out_weight),
            far(dt_weight),
            dt_bias[None, :],
            skip_weight[None, :],
        )
        for into, value in zip((gated, gz, gxs, gprojs, small, dtg, cots), got):
            into.append(value)
        gprojs[s] = sum_pair(gprojs[s], "fsdp")
        branch.append(RowScatter(*got[7:], "fsdp"))

    def run_leave(s, *behind):
        got = leave(
            offs,
            [far(term) for term in gprojs[s]],
            far(proj_weight),
            after(gxs[s], *behind),
            xin[s],
            xs[s],
            gz[s],
            masks[s],
            conv_weight,
            tap_bias,
            far(in_x_weight),
            far(in_z_weight),
            normed[s],
        )
        for into, value in zip((g_x_in, rows_part, proj_part, gain_part), got):
            into.append(value)
        gn.append(RowScatter(*got[4:], "fsdp"))

    def total_of(parts):
        total = [part.astype(f32) for part in parts]
        while len(total) > 1:
            total = [total[n] + total[n + 1] for n in range(0, len(total), 2)]
        return total[0]

    bits = [lax.rem(lax.axis_index("dp") // bit, 2) for bit in bits_of(dp)]
    place = jnp.stack(bits).astype(jnp.int32)
    scatter = GradScatter if dp == 8 and (model // dp) % 256 == 0 else PlainGradScatter
    run_enter(0)
    run_recurrence(0)
    branch[0].send()
    run_enter(1, gated[0])
    branch[0].mid()
    branch[0].send()
    run_leave(0, projs[1][0])
    gn[0].send()
    run_recurrence(1, g_x_in[0])
    branch[1].send()
    gate = (branch[0].got, gn[0].got)
    out_sum = scatter([cots], [[gated[0], after(gated[1], *gate)]], place)
    out_sum.send_core()
    z_sum = scatter([normed], [gz], place)
    z_sum.send_core()
    gn[0].mid()
    gn[0].send()
    out_sum.send_first()
    z_sum.send_first()
    branch[1].mid()
    branch[1].send()
    run_leave(1, out_sum.rest(), z_sum.rest())
    gn[1].send()
    out_sum.send_second(g_x_in[1])
    z_sum.send_second(out_sum.rest())
    x_sum = scatter([normed], [[g_x_in[0], after(g_x_in[1], z_sum.rest())]], place)
    x_sum.send_core()
    x_sum.send_first()
    gn[1].got = after(gn[1].got, x_sum.rest())
    gn[1].mid()
    gn[1].send()
    packed = jnp.concatenate(
        [sum(proj_part), sum(rows_part), sum(small), jnp.concatenate([sum(gain_part).reshape(-1, inner)] * 4, 0)], 0
    )
    packed = all_sum(after(packed, x_sum.rest()), "dp")
    x_sum.send_second(branch[1].got, out_sum.h1, out_sum.h2, z_sum.h1, z_sum.h2)
    gain_rows = packed[proj_weight.shape[0] + 16 : proj_weight.shape[0] + 16 + model // inner]
    gain_grad = total_of(exchange_all(gain_rows, "fsdp")).reshape(-1) / gain
    (out_grad,), (in_z_grad,), (in_x_grad,) = out_sum.finish(x_sum.rest()), z_sum.finish(x_sum.rest()), x_sum.finish()
    outputs, input_grads = [], []
    for s in seqs:
        v = after(states_in[s], x_sum.rest()).astype(f32)
        outputs.append((v + branch[s].finish()).astype(bf16))
        rscale = lax.rsqrt(jnp.mean(v * v, axis=1, keepdims=True) + norm_eps)
        scaled = gn[s].finish() * gain
        inner_mean = jnp.mean(scaled * v, axis=1, keepdims=True)
        input_grads.append(out_cotangent[s].astype(f32) + rscale * scaled - v * (rscale * rscale * rscale) * inner_mean)
    dt_grad = scatter_of(after(sum(dtg), x_sum.rest()), "dp").finish()
    tail = packed[proj_weight.shape[0] :]
    return (
        jnp.stack(outputs),
        jnp.stack(input_grads),
        gain_grad,
        in_x_grad,
        in_z_grad,
        tail[:span],
        tail[span],
        packed[: proj_weight.shape[0]].T,
        dt_grad,
        tail[8 + 1],
        tail[8],
        out_grad.T,
    )


def solution(mesh):
    in_specs = (
        P("dp", "fsdp", None),
        P("dp", "fsdp", None),
        P("dp", None),
        P("dp", None),
        P(),
        P(None, "fsdp"),
        P(None, "fsdp"),
        P(None, "fsdp"),
        P("fsdp"),
        P("fsdp", None),
        P(None, "fsdp"),
        P("fsdp"),
        P("fsdp"),
        P("fsdp", None),
    )
    out_specs = (
        P("dp", "fsdp", None),
        P("dp", "fsdp", None),
        P(),
        P("dp", "fsdp"),
        P("dp", "fsdp"),
        P(None, "fsdp"),
        P("fsdp"),
        P("fsdp", None),
        P("dp", "fsdp"),
        P("fsdp"),
        P("fsdp"),
        P("fsdp", "dp"),
    )
    return jax.shard_map(per_device, mesh=mesh, in_specs=in_specs, out_specs=out_specs, check_vma=False)
```

```python
import functools

import jax
import jax.numpy as jnp
from jax import lax
from jax.experimental import pallas as pl
from jax.experimental.pallas import tpu as pltpu
from jax.sharding import PartitionSpec as P

BLOCK = 16
LANES = 128
norm_eps = 1e-05


def takes(microseconds):
    return pl.CostEstimate(flops=int(microseconds * 9e8), bytes_accessed=1, transcendentals=0)
f32 = jnp.float32
bf16 = jnp.bfloat16


def mm(left, right, contract):
    return lax.dot_general(left, right, ((contract[:1], contract[1:]), ((), ())), preferred_element_type=f32)


def swap(x, axis, bit):
    return lax.ppermute(x, axis, [(i, i ^ bit) for i in range(lax.axis_size(axis))])


def bits_of(count):
    return [1 << k for k in range(count.bit_length() - 1)]


def exchange_all(x, axis):
    return [x] + [swap(x, axis, mask) for mask in range(1, lax.axis_size(axis))]


def relay_all(x, axis):
    held = {0: x}
    for bit in reversed(bits_of(lax.axis_size(axis))):
        for mask in list(held):
            held[mask | bit] = swap(held[mask], axis, bit)
    return [held[mask] for mask in range(len(held))]


class RowScatter:
    def __init__(self, sent, kept, axis):
        self.axis, self.bits = axis, bits_of(lax.axis_size(axis))
        self.sent, self.kept = sent, kept

    def send(self, *behind):
        self.got = swap(after(self.sent, *behind), self.axis, self.bits.pop(0))

    def mid(self):
        self.sent = (self.kept[1::2].astype(f32) + self.got[1::2].astype(f32)).astype(bf16)
        self.kept = (self.kept[0::2].astype(f32) + self.got[0::2].astype(f32))

    def finish(self):
        while self.bits:
            self.mid()
            self.send()
        return self.kept[0].astype(f32) + self.got[0].astype(f32)


def after(x, *others):
    return lax.optimization_barrier((x, others))[0] if others else x


def sum_pair(x, axis):
    bits = bits_of(lax.axis_size(axis))
    for bit in bits[:-1]:
        x = (x.astype(f32) + swap(x, axis, bit).astype(f32)).astype(bf16)
    return [x, swap(x, axis, bits[-1])]


def take_bit(x, dim, value):
    return lax.dynamic_index_in_dim(x, value, dim, keepdims=False)


class Scatter:
    def __init__(self, x, axis, bits, dims):
        self.x, self.axis, self.left = x, axis, list(zip(bits, dims))

    def send(self):
        bit, dim = self.left[0]
        own = (lax.axis_index(self.axis) // bit) % 2
        self.got = swap(take_bit(self.x, dim, 1 - own).astype(bf16), self.axis, bit)
        self.kept = take_bit(self.x, dim, own)
        return self.got

    def add(self):
        _, dim = self.left.pop(0)
        self.left = [(bit, d - 1 if d > dim else d) for bit, d in self.left]
        self.x = self.kept.astype(f32) + self.got.astype(f32)

    def finish(self):
        while self.left:
            self.send()
            self.add()
        return self.x


def scatter_of(x, axis):
    count = lax.axis_size(axis)
    bits = bits_of(count)
    n = len(bits)
    return Scatter(x.reshape((2,) * n + (x.shape[0] // count,) + x.shape[1:]), axis, bits, range(n - 1, -1, -1))


def all_sum(x, axis, kind=bf16):
    for bit in bits_of(lax.axis_size(axis)):
        low = x.astype(kind)
        x = low.astype(f32) + swap(low, axis, bit).astype(f32)
    return x


def far(x):
    return pltpu.with_memory_space_constraint(x, pltpu.HBM)


def add_up(refs):
    total = refs[0][...].astype(f32)
    for ref in refs[1:]:
        total = total + ref[...].astype(f32)
    return total


def silu_slope(v):
    s = jax.nn.sigmoid(v)
    return s * (1.0 + v * (1.0 - s))


def conv_sum(x, masks, taps, bias):
    span = taps.shape[0]
    total = bias + taps[span - 1 : span] * x
    shifted = []
    for w in range(span - 1):
        moved = pltpu.roll(x, span - 1 - w, 0) * masks[:, w : w + 1]
        shifted.append(moved)
        total = total + taps[w : w + 1] * moved
    return total, shifted + [x]


def enter_kernel(count, offs_ref, *refs):
    parts = refs[:count]
    gain_ref, mask_ref, wx_ref, wz_ref, taps_ref, bias_ref, wp_ref = refs[count : count + 7]
    normed_ref, xin_ref, z_ref, xs_ref, proj_ref, acc_s = refs[count + 7 :]
    step = pl.program_id(0)

    @pl.when(step == 0)
    def _():
        gain = gain_ref[...].astype(f32)
        for m, part in enumerate(parts):
            v = part[...].astype(f32)
            rscale = lax.rsqrt(jnp.mean(v * v, axis=1, keepdims=True) + norm_eps)
            rows = part.shape[0]
            normed_ref[pl.ds(pl.multiple_of(offs_ref[0, m], rows), rows), :] = (v * rscale * gain).astype(bf16)
        acc_s[...] = jnp.zeros_like(acc_s)

    normed = normed_ref[...]
    z_ref[...] = jnp.dot(normed, wz_ref[...], preferred_element_type=f32)
    x_in = jnp.dot(normed, wx_ref[...], preferred_element_type=f32).astype(bf16)
    xin_ref[...] = x_in
    pre, _ = conv_sum(x_in.astype(f32), mask_ref[...], taps_ref[...].astype(f32), bias_ref[...].astype(f32))
    xs = jax.nn.silu(pre).astype(bf16)
    xs_ref[...] = xs
    acc_s[...] += mm(wp_ref[...], xs, (1, 1))

    @pl.when(step == pl.num_programs(0) - 1)
    def _():
        proj_ref[...] = acc_s[...].astype(bf16)


def blocks_of(rows, wide):
    return pl.BlockSpec((rows, wide), lambda c: (0, c))


def whole_of(shape):
    return pl.BlockSpec(shape, lambda c: (0,) * len(shape))


def enter(offs, parts, gain, masks, wx, wz, taps, bias, wp):
    rows, model = parts[0].shape
    seq_len = rows * len(parts)
    inner = wx.shape[1]
    wide = 512
    return pl.pallas_call(
        functools.partial(enter_kernel, len(parts)),
        grid=(inner // wide,),
        in_specs=[pl.BlockSpec(memory_space=pltpu.SMEM)]
        + [whole_of((rows, model))] * len(parts)
        + [
            whole_of((1, model)),
            whole_of(masks.shape),
            blocks_of(model, wide),
            blocks_of(model, wide),
            blocks_of(taps.shape[0], wide),
            blocks_of(1, wide),
            blocks_of(wp.shape[0], wide),
        ],
        out_specs=[
            whole_of((seq_len, model)),
            blocks_of(seq_len, wide),
            blocks_of(seq_len, wide),
            blocks_of(seq_len, wide),
            whole_of((wp.shape[0], seq_len)),
        ],
        out_shape=[
            jax.ShapeDtypeStruct((seq_len, model), bf16),
            jax.ShapeDtypeStruct((seq_len, inner), bf16),
            jax.ShapeDtypeStruct((seq_len, inner), f32),
            jax.ShapeDtypeStruct((seq_len, inner), bf16),
            jax.ShapeDtypeStruct((wp.shape[0], seq_len), bf16),
        ],
        scratch_shapes=[pltpu.VMEM((wp.shape[0], seq_len), f32)],
        name="enter",
        compiler_params=pltpu.CompilerParams(vmem_limit_bytes=28 * 1024 * 1024),
        cost_estimate=takes(9),
    )(offs, *parts, gain, masks, wx, wz, taps, bias, wp)


def write_parts(offs_ref, total_s, sent_ref, kept_ref):
    count, rows = kept_ref.shape[0], kept_ref.shape[1]
    for m in range(count):
        for odd, out in ((0, kept_ref), (1, sent_ref)):
            off = pl.multiple_of(offs_ref[0, 2 * m + odd], rows)
            out[m] = total_s[pl.ds(off, rows), :].astype(bf16)


def leave_kernel(count, offs_ref, *refs):
    terms = refs[:count]
    wp_ref, gxs_ref, xin_ref, xs_ref, gz_ref, mask_ref, taps_ref, bias_ref, wx_ref, wz_ref, normed_ref = refs[
        count : count + 11
    ]
    gxin_ref, rows_ref, xpg_ref, gain_ref = refs[count + 11 : count + 15]
    sent_ref, kept_ref, acc_s = refs[count + 15 :]
    step = pl.program_id(0)
    span = taps_ref.shape[0]
    seq_len = xin_ref.shape[0]
    gproj = add_up(terms).astype(bf16)
    xpg_ref[...] = mm(gproj, xs_ref[...], (1, 0))
    g_xs = gxs_ref[...] + mm(gproj, wp_ref[...], (0, 0))
    masks = mask_ref[...]
    taps = taps_ref[...].astype(f32)
    pre, shifted = conv_sum(xin_ref[...].astype(f32), masks, taps, bias_ref[...].astype(f32))
    g_conv = g_xs * silu_slope(pre)
    total = taps[span - 1 : span] * g_conv
    for w in range(span):
        rows_ref[w : w + 1, :] = jnp.sum(g_conv * shifted[w], axis=0, keepdims=True)
        if w < span - 1:
            term = g_conv * masks[:, w : w + 1] * taps[w : w + 1]
            total = total + pltpu.roll(term, seq_len - (span - 1 - w), 0)
    rows_ref[span : span + 1, :] = jnp.sum(g_conv, axis=0, keepdims=True)
    rows_ref[span + 1 :, :] = jnp.zeros((8 - span - 1, g_conv.shape[1]), f32)
    g_x_in = total.astype(bf16)
    gxin_ref[...] = g_x_in
    gn = mm(g_x_in, wx_ref[...], (1, 1)) + mm(gz_ref[...], wz_ref[...], (1, 1))

    @pl.when(step == 0)
    def _():
        acc_s[...] = gn

    @pl.when(step > 0)
    def _():
        acc_s[...] += gn

    @pl.when(step == pl.num_programs(0) - 1)
    def _():
        gn = acc_s[...]
        write_parts(offs_ref, acc_s, sent_ref, kept_ref)
        gain_ref[...] = jnp.sum(gn * normed_ref[...].astype(f32), axis=0, keepdims=True)


def leave(offs, terms, wp, gxs, xin, xs, gz, masks, taps, bias, wx, wz, normed):
    seq_len, model = normed.shape
    inner = wx.shape[1]
    count = offs.shape[1]
    wide = 256
    return pl.pallas_call(
        functools.partial(leave_kernel, len(terms)),
        grid=(inner // wide,),
        in_specs=[pl.BlockSpec(memory_space=pltpu.SMEM)]
        + [whole_of(terms[0].shape)] * len(terms)
        + [
            blocks_of(wp.shape[0], wide),
            blocks_of(seq_len, wide),
            blocks_of(seq_len, wide),
            blocks_of(seq_len, wide),
            blocks_of(seq_len, wide),
            whole_of(masks.shape),
            blocks_of(taps.shape[0], wide),
            blocks_of(1, wide),
            blocks_of(model, wide),
            blocks_of(model, wide),
            whole_of((seq_len, model)),
        ],
        out_specs=[
            blocks_of(seq_len, wide),
            blocks_of(8, wide),
            blocks_of(wp.shape[0], wide),
            whole_of((1, model)),
        ]
        + [whole_of((count // 2, seq_len // count, model))] * 2,
        out_shape=[
            jax.ShapeDtypeStruct((seq_len, inner), bf16),
            jax.ShapeDtypeStruct((8, inner), f32),
            jax.ShapeDtypeStruct((wp.shape[0], inner), f32),
            jax.ShapeDtypeStruct((1, model), f32),
        ]
        + [jax.ShapeDtypeStruct((count // 2, seq_len // count, model), bf16)] * 2,
        scratch_shapes=[pltpu.VMEM((seq_len, model), f32)],
        name="leave",
        compiler_params=pltpu.CompilerParams(vmem_limit_bytes=24 * 1024 * 1024),
        cost_estimate=takes(10),
    )(offs, *terms, wp, gxs, xin, xs, gz, masks, taps, bias, wx, wz, normed)


def recurrence_kernel(state_dim, rank, count, keep_ref, offs_ref, *refs):
    parts, terms, refs = refs[:count], refs[count : count + 2], refs[count + 2 :]
    xs_ref, z_ref, wo_ref, wdt_ref, dtb_ref, skip_ref = refs[:6]
    gated_ref, gz_ref, gxs_ref, gproj_ref, small_ref, dtg_ref, cot_ref, sent_ref, kept_ref = refs[6:15]
    (
        gg_s,
        proj_s,
        gproj_s,
        acc_s,
        slope_s,
        eps_s,
        u_s,
        gm_s,
        y_s,
        s1_s,
        s2_s,
        hist_s,
        even_g_s,
        odd_g_s,
        even_p_s,
        odd_p_s,
        kt_s,
        qt_s,
        kd_s,
        k2d_s,
        qd_s,
        norm_s,
        sum_s,
        tail_s,
        gq_s,
        ge_s,
        pe_s,
        gqt_s,
        get_s,
        pet_s,
    ) = refs[15:]
    step = pl.program_id(0)
    seq_len, width = xs_ref.shape
    blocks = seq_len // BLOCK
    flat = BLOCK * state_dim
    lane = lax.broadcasted_iota(jnp.int32, (state_dim, BLOCK), 1)

    @pl.when(step == 0)
    def _():
        proj_s[...] = add_up(terms)
        for m, part in enumerate(parts):
            rows = part.shape[0]
            cot_ref[pl.ds(pl.multiple_of(offs_ref[0, m], rows), rows), :] = part[...]
        turned = proj_s[rank:, :]
        for b in range(blocks):
            cols = slice(b * BLOCK, (b + 1) * BLOCK)
            kt_s[b] = jnp.pad(turned[:state_dim, cols], ((0, 0), (0, LANES - BLOCK)))
            qt_s[b] = jnp.pad(turned[state_dim:, cols], ((0, 0), (0, LANES - BLOCK)))
        source = lax.broadcasted_iota(jnp.int32, (2 * state_dim, flat), 0)
        target = lax.rem(lax.broadcasted_iota(jnp.int32, (2 * state_dim, flat), 1), state_dim)
        take_k = (source == target).astype(bf16)
        take_q = (source == target + state_dim).astype(bf16)
        own = (
            lax.rem(lax.broadcasted_iota(jnp.int32, (seq_len, flat), 0), BLOCK)
            == lax.broadcasted_iota(jnp.int32, (seq_len, flat), 1) // state_dim
        )
        kd_s[...] = jnp.where(own, mm(turned.astype(bf16), take_k, (0, 0)), 0.0).astype(bf16)
        k2d_s[...] = jnp.where(own, mm((turned * turned).astype(bf16), take_k, (0, 0)), 0.0).astype(bf16)
        qd_s[...] = jnp.where(own, mm(turned.astype(bf16), take_q, (0, 0)), 0.0).astype(bf16)
        square = jnp.sum(turned[:state_dim] * turned[:state_dim], axis=0, keepdims=True)
        norm_s[...] = jnp.broadcast_to(square, (LANES, seq_len)).T
        sum_s[...] = jnp.zeros_like(sum_s)
        gq_s[...] = jnp.zeros_like(gq_s)
        ge_s[...] = jnp.zeros_like(ge_s)
        pe_s[...] = jnp.zeros_like(pe_s)

    gg_s[...] = mm(cot_ref[...], wo_ref[...], (1, 1))
    low = proj_s[:rank, :].astype(bf16)
    dt_pre = mm(low, wdt_ref[...], (0, 0)) + dtb_ref[...].astype(f32)
    rates = jnp.maximum(dt_pre, 0.0) + jnp.log1p(jnp.exp(-jnp.abs(dt_pre)))
    ratio = 1.0 / (1.0 + rates * norm_s[:, 0:1])
    eps_s[...] = rates * ratio
    slope_s[...] = ratio * ratio * jax.nn.sigmoid(dt_pre)
    u_s[...] = eps_s[...] * xs_ref[...].astype(f32)
    gm_s[...] = gg_s[...] * jax.nn.silu(z_ref[...])
    hist_s[0:state_dim, :] = jnp.zeros((state_dim, width), bf16)

    def own_token(pairs):
        picked = pairs[:state_dim]
        for t in range(1, BLOCK):
            picked = jnp.where(lane == t, pairs[t * state_dim : (t + 1) * state_dim], picked)
        return picked

    def read_states(b, buf):
        toks = pl.ds(pl.multiple_of(b * BLOCK, BLOCK), BLOCK)
        hblk = buf[...]
        y_s[toks, :] = jnp.dot(qd_s[toks, :], hblk, preferred_element_type=f32)
        gqt_s[b, :, :BLOCK] = own_token(mm(hblk, gm_s[toks, :].astype(bf16), (1, 1)))

    def scan_block(b, h, buf):
        base = pl.multiple_of(b * BLOCK, BLOCK)
        kt = kt_s[b]
        for t in range(BLOCK):
            if t % 8 == 0:
                h = h * keep_ref[0, b * 2 + t // 8]
            col = jnp.broadcast_to(kt[:, t : t + 1], (state_dim, width))
            e = eps_s[pl.ds(base + t, 1), :]
            u = u_s[pl.ds(base + t, 1), :]
            h = (1.0 - (col * col) * e) * h + col * u
            kept = h.astype(bf16)
            hist_s[pl.ds(pl.multiple_of((base + t + 1) * state_dim, state_dim), state_dim), :] = kept
            buf[t * state_dim : (t + 1) * state_dim, :] = kept
        return h

    def forward(i, h):
        read_states(jnp.maximum(2 * i - 1, 0), odd_g_s)
        h = scan_block(2 * i, h, even_g_s)
        read_states(2 * i, even_g_s)
        return scan_block(2 * i + 1, h, odd_g_s)

    lax.fori_loop(0, blocks // 2, forward, jnp.zeros((state_dim, width), f32))
    read_states(blocks - 1, odd_g_s)

    def read_grads(b, gbuf, pbuf):
        toks = pl.ds(pl.multiple_of(b * BLOCK, BLOCK), BLOCK)
        gblk = gbuf[...]
        pblk = pbuf[...]
        s1_s[toks, :] = jnp.dot(kd_s[toks, :], gblk, preferred_element_type=f32)
        s2_s[toks, :] = jnp.dot(k2d_s[toks, :], pblk, preferred_element_type=f32)
        get_s[b, :, :BLOCK] = own_token(mm(gblk, u_s[toks, :].astype(bf16), (1, 1)))
        pet_s[b, :, :BLOCK] = own_token(mm(pblk, eps_s[toks, :].astype(bf16), (1, 1)))

    def back_block(b, carry, gbuf, pbuf):
        base = pl.multiple_of(b * BLOCK, BLOCK)
        kt = kt_s[b]
        qt = qt_s[b]
        for t in reversed(range(BLOCK)):
            colq = jnp.broadcast_to(qt[:, t : t + 1], (state_dim, width))
            col = jnp.broadcast_to(kt[:, t : t + 1], (state_dim, width))
            e = eps_s[pl.ds(base + t, 1), :]
            gm = gm_s[pl.ds(base + t, 1), :]
            g = colq * gm + carry
            before = hist_s[pl.ds(pl.multiple_of((base + t) * state_dim, state_dim), state_dim), :].astype(f32)
            p = g * before
            carry = (1.0 - (col * col) * e) * g
            if t % 8 == 0:
                k = keep_ref[0, b * 2 + t // 8]
                carry = carry * k
                p = p * k
            gbuf[t * state_dim : (t + 1) * state_dim, :] = g.astype(bf16)
            pbuf[t * state_dim : (t + 1) * state_dim, :] = p.astype(bf16)
        return carry

    def backward(i, carry):
        last = blocks - 1 - 2 * i
        read_grads(jnp.minimum(last + 1, blocks - 1), even_g_s, even_p_s)
        carry = back_block(last, carry, odd_g_s, odd_p_s)
        read_grads(last, odd_g_s, odd_p_s)
        return back_block(last - 1, carry, even_g_s, even_p_s)

    lax.fori_loop(0, blocks // 2, backward, jnp.zeros((state_dim, width), f32))
    read_grads(0, even_g_s, even_p_s)
    gq_s[...] += gqt_s[...]
    ge_s[...] += get_s[...]
    pe_s[...] += pet_s[...]

    xs = xs_ref[...].astype(f32)
    z = z_ref[...]
    skip = skip_ref[...].astype(f32)
    sig = jax.nn.sigmoid(z)
    mixed = y_s[...] + skip * xs
    gated = (mixed * (z * sig)).astype(bf16)
    gated_ref[...] = gated
    out_part = jnp.dot(gated, wo_ref[...], preferred_element_type=f32)
    gz_ref[...] = (gg_s[...] * mixed * (sig * (1.0 + z * (1.0 - sig)))).astype(bf16)
    gm = gm_s[...]
    s1 = s1_s[...]
    eps = eps_s[...]
    g_eps = xs * s1 - s2_s[...]
    sum_s[...] += jnp.broadcast_to(jnp.sum(g_eps * eps * eps, axis=1, keepdims=True), sum_s.shape)
    g_dt = (g_eps * slope_s[...]).astype(bf16)
    dtg_ref[...] = mm(low, g_dt, (1, 0))
    gxs_ref[...] = skip * gm + eps * s1
    small_ref[0:1, :] = jnp.sum(gm * xs, axis=0, keepdims=True)
    small_ref[1:2, :] = jnp.sum(g_dt.astype(f32), axis=0, keepdims=True)
    small_ref[2:, :] = jnp.zeros((6, width), f32)
    g_low = mm(wdt_ref[...], g_dt, (1, 1))

    @pl.when(step == 0)
    def _():
        gproj_s[...] = g_low
        acc_s[...] = out_part

    @pl.when(step > 0)
    def _():
        gproj_s[...] += g_low
        acc_s[...] += out_part

    @pl.when(step == pl.num_programs(0) - 1)
    def _():
        scale = sum_s[...].T[0:1, :]
        for b in range(blocks):
            cols = slice(b * BLOCK, (b + 1) * BLOCK)
            own_keys = ge_s[b, :, :BLOCK] - 2.0 * kt_s[b, :, :BLOCK] * (pe_s[b, :, :BLOCK] + scale[:, cols])
            tail_s[:state_dim, cols] = own_keys
            tail_s[state_dim:, cols] = gq_s[b, :, :BLOCK]
        gproj_ref[:rank, :] = gproj_s[...].astype(bf16)
        gproj_ref[rank:, :] = tail_s[...].astype(bf16)
        write_parts(offs_ref, acc_s, sent_ref, kept_ref)


def recurrence(keep, offs, parts, terms, xs, z, wo, wdt, dt_bias, skip):
    seq_len, inner = xs.shape
    model = wo.shape[1]
    rank = wdt.shape[0]
    columns = terms[0].shape[0]
    state_dim = (columns - rank) // 2
    wide = 512
    flat = BLOCK * state_dim
    blocks = seq_len // BLOCK
    vmem = pltpu.VMEM
    return pl.pallas_call(
        functools.partial(recurrence_kernel, state_dim, rank, len(parts)),
        grid=(inner // wide,),
        in_specs=[pl.BlockSpec(memory_space=pltpu.SMEM)] * 2
        + [whole_of(parts[0].shape)] * len(parts)
        + [whole_of((columns, seq_len))] * len(terms)
        + [
            blocks_of(seq_len, wide),
            blocks_of(seq_len, wide),
            pl.BlockSpec((wide, model), lambda c: (c, 0)),
            blocks_of(rank, wide),
            blocks_of(1, wide),
            blocks_of(1, wide),
        ],
        out_specs=[
            blocks_of(seq_len, wide),
            blocks_of(seq_len, wide),
            blocks_of(seq_len, wide),
            whole_of((columns, seq_len)),
            blocks_of(8, wide),
            blocks_of(rank, wide),
            whole_of((seq_len, model)),
        ]
        + [whole_of((len(parts) // 2,) + parts[0].shape)] * 2,
        out_shape=[
            jax.ShapeDtypeStruct((seq_len, inner), bf16),
            jax.ShapeDtypeStruct((seq_len, inner), bf16),
            jax.ShapeDtypeStruct((seq_len, inner), f32),
            jax.ShapeDtypeStruct((columns, seq_len), bf16),
            jax.ShapeDtypeStruct((8, inner), f32),
            jax.ShapeDtypeStruct((rank, inner), f32),
            jax.ShapeDtypeStruct((seq_len, model), bf16),
        ]
        + [jax.ShapeDtypeStruct((len(parts) // 2,) + parts[0].shape, bf16)] * 2,
        scratch_shapes=[
            vmem((seq_len, wide), f32),
            vmem((columns, seq_len), f32),
            vmem((rank, seq_len), f32),
            vmem((seq_len, model), f32),
            vmem((seq_len, wide), f32),
        ]
        + [vmem((seq_len, wide), f32)] * 6
        + [vmem(((seq_len + 1) * state_dim, wide), bf16)]
        + [vmem((flat, wide), bf16)] * 4
        + [vmem((blocks, state_dim, LANES), f32)] * 2
        + [vmem((seq_len, flat), bf16)] * 3
        + [vmem((seq_len, LANES), f32)] * 2
        + [vmem((2 * state_dim, seq_len), f32)]
        + [vmem((blocks, state_dim, LANES), f32)] * 6,
        name="recurrence",
        compiler_params=pltpu.CompilerParams(vmem_limit_bytes=30 * 1024 * 1024),
        cost_estimate=takes(30),
    )(keep, offs, *parts, *terms, xs, z, wo, wdt, dt_bias, skip)


def grad_of(lefts, rights):
    total = mm(lefts[0][...], rights[0][...], (0, 0))
    for left, right in zip(lefts[1:], rights[1:]):
        total = total + mm(left[...], right[...], (0, 0))
    return total


def grad_send_kernel(pairs, count, place_ref, *refs):
    out_ref = refs[2 * pairs * count]
    for g in range(pairs):
        lefts = refs[g * count : (g + 1) * count]
        rights = refs[(pairs + g) * count : (pairs + g + 1) * count]
        out_ref[g, 0] = grad_of(lefts, rights).astype(bf16)


def grad_keep_kernel(pairs, count, place_ref, *refs):
    got_ref, t1_ref, k1_ref, t2_ref, k2_ref = refs[2 * pairs * count :]
    half = t1_ref.shape[2]
    own_y = pl.program_id(0) == 1
    own_x = pl.program_id(1) == 1
    for g in range(pairs):
        lefts = refs[g * count : (g + 1) * count]
        rights = refs[(pairs + g) * count : (pairs + g + 1) * count]
        total = (grad_of(lefts, rights) + got_ref[g, 0].astype(f32)).astype(bf16)

        @pl.when(own_x)
        def _():
            k1_ref[g, 0] = total[:half]

        @pl.when(jnp.logical_not(own_x))
        def _():
            t1_ref[g, 0] = total[:half]

        @pl.when(own_y)
        def _():
            k2_ref[g, 0] = total[half:]

        @pl.when(jnp.logical_not(own_y))
        def _():
            t2_ref[g, 0] = total[half:]


def grad_mid_kernel(place_ref, k1_ref, g1_ref, k2_ref, g2_ref, o1_ref, m1_ref, o2_ref, m2_ref):
    x, y = place_ref[1], place_ref[2]
    for g in range(k1_ref.shape[0]):
        for kept, got, out, mine, own in (
            (k1_ref, g1_ref, o1_ref, m1_ref, y),
            (k2_ref, g2_ref, o2_ref, m2_ref, x),
        ):
            out[g] = (kept[g, 1 - own].astype(f32) + got[g, 1 - own].astype(f32)).astype(bf16)
            mine[g] = kept[g, own].astype(f32) + got[g, own].astype(f32)


class GradScatter:
    def __init__(self, lefts, rights, place):
        self.lefts, self.rights, self.place = lefts, rights, place
        self.pairs, self.count = len(lefts), len(lefts[0])
        self.flat = [a for pair in lefts for a in pair] + [a for pair in rights for a in pair]
        seq_len, model = lefts[0][0].shape
        self.inner = rights[0][0].shape[1]
        self.seq_len, self.rows = seq_len, model // 8

    def specs(self, index):
        n = self.pairs * self.count
        lhs = pl.BlockSpec((self.seq_len, self.rows), index)
        rhs = pl.BlockSpec((self.seq_len, self.inner), lambda *_: (0, 0))
        return [lhs] * n + [rhs] * n

    def send_core(self):
        self.got = swap(
            pl.pallas_call(
                functools.partial(grad_send_kernel, self.pairs, self.count),
                grid_spec=pltpu.PrefetchScalarGridSpec(
                    num_scalar_prefetch=1,
                    grid=(4,),
                    in_specs=self.specs(lambda j, place: (0, 2 * j + 1 - place[0])),
                    out_specs=pl.BlockSpec((self.pairs, 1, self.rows, self.inner), lambda j, place: (0, j, 0, 0)),
                ),
                out_shape=jax.ShapeDtypeStruct((self.pairs, 4, self.rows, self.inner), bf16),
                name="grad_send",
            compiler_params=pltpu.CompilerParams(vmem_limit_bytes=12 * 1024 * 1024),
                cost_estimate=takes(5.5),
            )(self.place, *self.flat),
            "dp",
            1,
        )

    def send_first(self, *behind):
        half = self.rows // 2
        shape = (self.pairs, 2, half, self.inner)
        block = (self.pairs, 1, half, self.inner)

        def at(i, own):
            return (1 - own) + i * (2 * own - 1)

        kinds = jax.ShapeDtypeStruct(shape, bf16)
        t1, self.k1, t2, self.k2 = pl.pallas_call(
            functools.partial(grad_keep_kernel, self.pairs, self.count),
            grid_spec=pltpu.PrefetchScalarGridSpec(
                num_scalar_prefetch=1,
                grid=(2, 2),
                in_specs=self.specs(lambda i, j, p: (0, 4 * at(i, p[2]) + 2 * at(j, p[1]) + p[0]))
                + [
                    pl.BlockSpec(
                        (self.pairs, 1, self.rows, self.inner),
                        lambda i, j, p: (0, 2 * at(i, p[2]) + at(j, p[1]), 0, 0),
                    )
                ],
                out_specs=[
                    pl.BlockSpec(block, lambda i, j, p: (0, at(i, p[2]), 0, 0)),
                    pl.BlockSpec(block, lambda i, j, p: (0, at(i, p[2]), 0, 0)),
                    pl.BlockSpec(block, lambda i, j, p: (0, at(jnp.maximum(i, j), p[1]), 0, 0)),
                    pl.BlockSpec(block, lambda i, j, p: (0, at(jnp.minimum(i, j), p[1]), 0, 0)),
                ],
            ),
            out_shape=[kinds] * 4,
            name="grad_keep",
            compiler_params=pltpu.CompilerParams(vmem_limit_bytes=14 * 1024 * 1024),
            cost_estimate=takes(6.5),
        )(self.place, *self.flat, after(self.got, *behind))
        self.left = self.k1
        self.g1, self.g2 = swap(t1, "dp", 2), swap(t2, "dp", 4)

    def rest(self):
        return self.left

    def send_second(self, *behind):
        half = self.rows // 2
        shape = (self.pairs, half, self.inner)
        whole = pl.BlockSpec((self.pairs, 2, half, self.inner), lambda i, p: (0, 0, 0, 0))
        part = pl.BlockSpec(shape, lambda i, p: (0, 0, 0))
        o1, self.m1, o2, self.m2 = pl.pallas_call(
            grad_mid_kernel,
            grid_spec=pltpu.PrefetchScalarGridSpec(
                num_scalar_prefetch=1, grid=(1,), in_specs=[whole] * 4, out_specs=[part] * 4
            ),
            out_shape=[jax.ShapeDtypeStruct(shape, kind) for kind in (bf16, f32, bf16, f32)],
            name="grad_mid",
            compiler_params=pltpu.CompilerParams(vmem_limit_bytes=8 * 1024 * 1024),
            cost_estimate=takes(3.5),
        )(self.place, after(self.k1, *behind), self.g1, self.k2, self.g2)
        self.left = self.m1
        self.h1, self.h2 = swap(o1, "dp", 4), swap(o2, "dp", 2)

    def finish(self, *behind):
        self.m1, self.m2, self.h1, self.h2 = after((self.m1, self.m2, self.h1, self.h2), *behind)
        return [
            jnp.concatenate([self.m1[g] + self.h1[g].astype(f32), self.m2[g] + self.h2[g].astype(f32)], 0)
            for g in range(self.pairs)
        ]


class PlainGradScatter:
    h1 = h2 = ()

    def __init__(self, lefts, rights, place):
        self.lefts, self.rights = lefts, rights

    def send_core(self):
        grads = [sum(mm(a, b, (0, 0)) for a, b in zip(left, right)) for left, right in zip(self.lefts, self.rights)]
        self.parts = [scatter_of(grad, "dp") for grad in grads]
        for part in self.parts:
            self.got = part.send()

    def send_first(self, *behind):
        for part in self.parts:
            part.add()
        for part in self.parts:
            part.send()

    send_second = send_first

    def rest(self):
        return self.parts[0].kept

    def finish(self, *behind):
        for part in self.parts:
            part.add()
        return [part.finish() for part in self.parts]


def per_device(
    states_in,
    out_cotangent,
    segments,
    starts,
    norm_gain,
    in_x_weight,
    in_z_weight,
    conv_weight,
    conv_bias,
    x_proj_weight,
    dt_weight,
    dt_bias,
    skip_weight,
    out_weight,
):
    count, rows, model = states_in.shape
    span, inner = conv_weight.shape
    rank = dt_weight.shape[0]
    seq_len = segments.shape[1]
    dp = lax.axis_size("dp")
    gain = norm_gain.astype(f32)
    proj_weight = x_proj_weight.T
    keep = 1.0 - starts[:, ::8].astype(f32)
    seqs = range(count)
    me = lax.axis_index("fsdp")
    offs = jnp.stack([(me ^ mask) * rows for mask in range(lax.axis_size("fsdp"))])[None, :].astype(jnp.int32)
    tap_bias = conv_bias[None, :]
    normed, xin, xs, z, masks, projs = [], [], [], [], [], []
    gated, gz, gxs, gprojs, small, dtg, cots, branch = [], [], [], [], [], [], [], []
    g_x_in, gn, rows_part, proj_part, gain_part = [], [], [], [], []
    tokens, cot_parts = [], []
    behind = ()
    for s in seqs:
        for source, into in ((states_in, tokens), (out_cotangent, cot_parts)):
            gather = relay_all if behind else exchange_all
            into.append(gather(after(source[s], *behind), "fsdp"))
            behind = (into[s][1],)
    for s in seqs:
        seg_ext = jnp.pad(segments[s], (span - 1, 0), constant_values=-1)
        mask = jnp.stack([(seg_ext[w : w + seq_len] == segments[s]).astype(f32) for w in range(span)], 1)
        masks.append(jnp.pad(mask, ((0, 0), (0, LANES - span))))

    def run_enter(s, *behind):
        got = enter(
            offs,
            [far(part) for part in tokens[s]],
            norm_gain[None, :],
            after(masks[s], *behind),
            far(in_x_weight),
            far(in_z_weight),
            conv_weight,
            tap_bias,
            far(proj_weight),
        )
        for into, value in zip((normed, xin, z, xs), got):
            into.append(value)
        projs.append(sum_pair(got[4], "fsdp"))

    def run_recurrence(s, *behind):
        got = recurrence(
            keep[s : s + 1],
            offs,
            [far(part) for part in cot_parts[s]],
            [far(term) for term in projs[s]],
            after(xs[s], *behind),
            z[s],
            far(out_weight),
            far(dt_weight),
            dt_bias[None, :],
            skip_weight[None, :],
        )
        for into, value in zip((gated, gz, gxs, gprojs, small, dtg, cots), got):
            into.append(value)
        gprojs[s] = sum_pair(gprojs[s], "fsdp")
        branch.append(RowScatter(*got[7:], "fsdp"))

    def run_leave(s, *behind):
        got = leave(
            offs,
            [far(term) for term in gprojs[s]],
            far(proj_weight),
            after(gxs[s], *behind),
            xin[s],
            xs[s],
            gz[s],
            masks[s],
            conv_weight,
            tap_bias,
            far(in_x_weight),
            far(in_z_weight),
            normed[s],
        )
        for into, value in zip((g_x_in, rows_part, proj_part, gain_part), got):
            into.append(value)
        gn.append(RowScatter(*got[4:], "fsdp"))

    def total_of(parts):
        total = [part.astype(f32) for part in parts]
        while len(total) > 1:
            total = [total[n] + total[n + 1] for n in range(0, len(total), 2)]
        return total[0]

    bits = [lax.rem(lax.axis_index("dp") // bit, 2) for bit in bits_of(dp)]
    place = jnp.stack(bits).astype(jnp.int32)
    scatter = GradScatter if dp == 8 and (model // dp) % 256 == 0 else PlainGradScatter
    run_enter(0)
    run_recurrence(0)
    branch[0].send()
    run_enter(1, gated[0])
    branch[0].mid()
    branch[0].send()
    run_leave(0, projs[1][0])
    gn[0].send()
    run_recurrence(1, g_x_in[0])
    branch[1].send()
    gate = (branch[0].got, gn[0].got)
    out_sum = scatter([cots], [[gated[0], after(gated[1], *gate)]], place)
    out_sum.send_core()
    z_sum = scatter([normed], [gz], place)
    z_sum.send_core()
    gn[0].mid()
    gn[0].send()
    out_sum.send_first()
    z_sum.send_first()
    branch[1].mid()
    branch[1].send()
    run_leave(1, out_sum.rest(), z_sum.rest())
    gn[1].send()
    out_sum.send_second(g_x_in[1])
    z_sum.send_second(out_sum.rest())
    x_sum = scatter([normed], [[g_x_in[0], after(g_x_in[1], z_sum.rest())]], place)
    x_sum.send_core()
    x_sum.send_first()
    gn[1].got = after(gn[1].got, x_sum.rest())
    gn[1].mid()
    gn[1].send()
    packed = jnp.concatenate(
        [sum(proj_part), sum(rows_part), sum(small), jnp.concatenate([sum(gain_part).reshape(-1, inner)] * 4, 0)], 0
    )
    packed = all_sum(after(packed, x_sum.rest()), "dp")
    x_sum.send_second(branch[1].got, out_sum.h1, out_sum.h2, z_sum.h1, z_sum.h2)
    gain_rows = packed[proj_weight.shape[0] + 16 : proj_weight.shape[0] + 16 + model // inner]
    gain_grad = total_of(exchange_all(gain_rows, "fsdp")).reshape(-1) / gain
    (out_grad,), (in_z_grad,), (in_x_grad,) = out_sum.finish(x_sum.h1), z_sum.finish(x_sum.h1), x_sum.finish()
    outputs, input_grads = [], []
    for s in seqs:
        v = after(states_in[s], x_sum.rest()).astype(f32)
        outputs.append((v + branch[s].finish()).astype(bf16))
        rscale = lax.rsqrt(jnp.mean(v * v, axis=1, keepdims=True) + norm_eps)
        scaled = gn[s].finish() * gain
        inner_mean = jnp.mean(scaled * v, axis=1, keepdims=True)
        input_grads.append(out_cotangent[s].astype(f32) + rscale * scaled - v * (rscale * rscale * rscale) * inner_mean)
    dt_grad = scatter_of(after(sum(dtg), x_sum.rest()), "dp").finish()
    tail = packed[proj_weight.shape[0] :]
    return (
        jnp.stack(outputs),
        jnp.stack(input_grads),
        gain_grad,
        in_x_grad,
        in_z_grad,
        tail[:span],
        tail[span],
        packed[: proj_weight.shape[0]].T,
        dt_grad,
        tail[8 + 1],
        tail[8],
        out_grad.T,
    )


def solution(mesh):
    in_specs = (
        P("dp", "fsdp", None),
        P("dp", "fsdp", None),
        P("dp", None),
        P("dp", None),
        P(),
        P(None, "fsdp"),
        P(None, "fsdp"),
        P(None, "fsdp"),
        P("fsdp"),
        P("fsdp", None),
        P(None, "fsdp"),
        P("fsdp"),
        P("fsdp"),
        P("fsdp", None),
    )
    out_specs = (
        P("dp", "fsdp", None),
        P("dp", "fsdp", None),
        P(),
        P("dp", "fsdp"),
        P("dp", "fsdp"),
        P(None, "fsdp"),
        P("fsdp"),
        P("fsdp", None),
        P("dp", "fsdp"),
        P("fsdp"),
        P("fsdp"),
        P("fsdp", "dp"),
    )
    return jax.shard_map(per_device, mesh=mesh, in_specs=in_specs, out_specs=out_specs, check_vma=False)
```
